512 devices in a mesh: dp: 8 (over z), expert: 64 (over x, y, core).
Axes of the slice: x: 4, y: 8, z: 8, core: 2. Of those that a mesh axis runs over, the one named last changes fastest.
Arguments:
- tokens: bfloat16 [65536, 1024], P(('dp', 'expert')), may hold values from -6 to 6
- d_output: bfloat16 [65536, 1024], P(('dp', 'expert')), may hold values from -6 to 6
- combine: float32 [65536, 8], P(('dp', 'expert')), may hold values from 0.05 to 1
- routes: int32 [65536, 8], P(('dp', 'expert')), may hold values from 0 to 63, all different within a row; in each aligned block of 128 rows (0 to 127, 128 to 255, ...) at most 18 rows name the same one
- gate_weight: bfloat16 [64, 1024, 384], P('expert', 'dp'), may hold values from -0.1875 to 0.1875
- up_weight: bfloat16 [64, 1024, 384], P('expert', 'dp'), may hold values from -0.1875 to 0.1875
- down_weight: bfloat16 [64, 384, 1024], P('expert', None, 'dp'), may hold values from -0.3125 to 0.3125
Outputs:
- d_tokens: bfloat16 [65536, 1024], P(('dp', 'expert'))
- d_gate_weight: float32 [64, 1024, 384], P('expert', 'dp')
- d_up_weight: float32 [64, 1024, 384], P('expert', 'dp')
- d_down_weight: float32 [64, 384, 1024], P('expert', None, 'dp')
The draws below stay inside these ranges and needn't reach their ends.
Inputs may be any that keep to these rules, and one draw needn't show every extreme that they name: `routes`: among the 128 tokens of one device, each expert id is named by at most 18 rows; some expert is named by exactly 18 rows on some device. The ids of one token differ.
All inputs are finite; a program needn't handle non-finite values.
Results may differ from the reference program's by a relative error of at most 0.015.
Values may be sent and summed in bfloat16 or wider, within the bound.
A program may use at most 64 MiB of HBM per device.

```python
import math
import jax
import jax.numpy as jnp
import numpy as np
from jax import lax

D = 1024
H = 384
TOP = 8
TOK_DEV = 128
EXPERTS = 64
CAP = 18
TOKENS = 65536
N_DP = 8
N_EXPERT = 64


def level_of(key, dims, split, smallest, high):
    def one(dim, shards_of):
        draws = jax.random.uniform(jax.random.fold_in(jax.random.fold_in(key, 6), dim), (shards_of,), jnp.float32, smallest / len(split), high / len(split))
        return jnp.repeat(jnp.exp(draws), dims[dim] // shards_of).reshape((-1,) + (1,) * (len(dims) - dim - 1))

    gain = one(*split[0])
    for cut in split[1:]:
        gain = gain * one(*cut)
    return gain


def shared_out(rng, own, number, rows, count, top, limit, slope):
    sequence = jax.random.permutation(rng, count)
    crowded, ordinary = load_shares(count, rows * top, limit, slope, True), load_shares(count, rows * top, limit, slope, False)
    places = jnp.arange(count)

    def named(sizes, rotation):
        used = int((sizes > 0).sum())
        fixed = max(1, used // 4)
        passed = fixed + (places - fixed + rotation * (used - fixed)) % max(1, count - fixed)
        return jnp.zeros((count,), jnp.int32).at[sequence[jnp.where(places < fixed, places, passed)]].set(jnp.asarray(sizes, jnp.int32))

    sizes = jnp.where(number % 4 == 0, named(crowded, number // 4), named(ordinary, number - number // 4 - 1))
    mixed = jax.random.permutation(jax.random.fold_in(own, 3), count)
    giver, receiver = mixed[0:count // 2 * 2:2], mixed[1:count // 2 * 2:2]
    room = jnp.minimum(sizes[giver] - 1, limit - sizes[receiver]) // 2
    room = jnp.where((giver == sequence[0]) | (receiver == sequence[0]) | (sizes[receiver] == 0), 0, jnp.maximum(room, 0))
    passed = jax.random.randint(jax.random.fold_in(own, 4), (count // 2,), 0, 1 << 20) % (room + 1)
    sizes = sizes.at[giver].add(-passed).at[receiver].add(passed)
    items = jnp.searchsorted(jnp.cumsum(sizes), jnp.arange(rows * top), side="right").astype(jnp.int32)
    listing = items.reshape(top, rows).T
    listing = listing[jax.random.permutation(jax.random.fold_in(own, 1), rows)]
    rotation = jax.random.randint(jax.random.fold_in(own, 2), (rows, 1), 0, top)
    return jnp.take_along_axis(listing, (jnp.arange(top)[None, :] + rotation) % top, axis=1)


def load_shares(number_of, total, reach, lean, full):
    weights = [(1 << 20) // math.isqrt(standing ** lean) + 1 for standing in range(1, number_of + 1)]
    largest = reach if full else min(reach, max(-(-total // number_of), total * weights[0] // sum(weights)))
    least = 1 if total - largest >= number_of - 1 else 0
    counts, rest = [largest] + [least] * (number_of - 1), total - largest - least * (number_of - 1)
    while rest > 0:
        candidates = [i for i in range(1, number_of) if counts[i] < largest] or [i for i in range(1, number_of) if counts[i] < reach]
        pool, left = sum([weights[i] for i in candidates]), rest
        for i in candidates:
            addition = min(reach - counts[i], max(1, left * weights[i] // pool), rest)
            counts[i] = counts[i] + addition
            rest = rest - addition
    return np.array(counts)


def normal_values(key, extent, width, limit, shards=(), kind=jnp.bfloat16):
    drawn = width * jax.random.normal(key, extent, jnp.float32)
    if shards:
        drawn = drawn * level_of(key, extent, shards, -0.22, 0.18)
    return jnp.clip(drawn, -limit, limit).astype(kind)


def setup_inputs(seed: int = 0) -> dict:
    keys = jax.random.split(jax.random.key(seed), 8)
    tokens = normal_values(keys[0], (TOKENS, D), 1.0, 6.0, ((0, 512),))
    d_output = normal_values(keys[1], (TOKENS, D), 1.0, 6.0, ((0, 512),))
    combine = jnp.clip(jnp.exp(math.log(1.0) - 2.9957323 * jax.random.uniform(keys[2], (TOKENS, TOP), jnp.float32) ** level_of(keys[2], (TOKENS, TOP), ((0, 512),), -0.2, 0.2)), 0.05, 1.0)
    routes_keys = jax.random.split(jax.random.fold_in(keys[3], 1), TOKENS // TOK_DEV)
    routes_turns = jax.random.permutation(jax.random.fold_in(keys[3], 3), TOKENS // TOK_DEV)
    routes = jax.vmap(lambda own, number: shared_out(jax.random.fold_in(keys[3], 2), own, number, TOK_DEV, EXPERTS, TOP, CAP, 1))(routes_keys, routes_turns).reshape((TOKENS, TOP))
    gate_weight = normal_values(keys[4], (EXPERTS, D, H), D ** -0.5, 0.1875, ((0, 64), (1, 8)))
    up_weight = normal_values(keys[5], (EXPERTS, D, H), D ** -0.5, 0.1875, ((0, 64), (1, 8)))
    down_weight = normal_values(keys[6], (EXPERTS, H, D), H ** -0.5, 0.3125, ((0, 64), (2, 8)))
    return dict(tokens=tokens, d_output=d_output, combine=combine, routes=routes, gate_weight=gate_weight, up_weight=up_weight, down_weight=down_weight)


def route_slots(routes, experts):
    matches = (routes[:, :, None] == jnp.arange(experts, dtype=jnp.int32)[None, None, :]).astype(jnp.int32)
    per_token = jnp.sum(matches, axis=1)
    earlier = jnp.cumsum(per_token, axis=0) - per_token
    return jnp.sum(matches * earlier[:, None, :], axis=2).astype(jnp.int32)


def row_work(row_inputs, row_grads, gate_up, down_matrix):
    hidden_units = down_matrix.shape[0]
    preact = jnp.dot(row_inputs, gate_up, preferred_element_type=jnp.float32)
    gate_pre = preact[:, :hidden_units]
    up_pre = preact[:, hidden_units:]
    gate_sigmoid = jax.nn.sigmoid(gate_pre)
    hidden = (gate_pre * gate_sigmoid * up_pre).astype(jnp.bfloat16)
    d_hidden = jnp.dot(row_grads, down_matrix.T, preferred_element_type=jnp.float32)
    d_gate_pre = d_hidden * up_pre * gate_sigmoid * (1.0 + gate_pre * (1.0 - gate_sigmoid))
    d_up_pre = d_hidden * gate_pre * gate_sigmoid
    d_preact = jnp.concatenate([d_gate_pre, d_up_pre], axis=1).astype(jnp.bfloat16)
    d_rows = jnp.dot(d_preact, gate_up.T, preferred_element_type=jnp.float32).astype(jnp.bfloat16)
    return d_rows, hidden, d_preact


def expert_grads(row_inputs, row_grads, hidden, d_preact):
    gate_up_grad = jnp.dot(row_inputs.T, d_preact, preferred_element_type=jnp.float32)
    down_grad = jnp.dot(row_grads.T, hidden, preferred_element_type=jnp.float32)
    return jnp.concatenate([gate_up_grad, down_grad], axis=1)


def reference(tokens, d_output, combine, routes, gate_weight, up_weight, down_weight):
    gate_up = jnp.concatenate([gate_weight, up_weight], axis=2)
    tok_groups = tokens.reshape(N_DP, N_EXPERT, TOK_DEV, D)
    grad_groups = d_output.reshape(N_DP, N_EXPERT, TOK_DEV, D)
    combine_groups = combine.reshape(N_DP, N_EXPERT, TOK_DEV, TOP)
    route_groups = routes.reshape(N_DP, N_EXPERT, TOK_DEV, TOP)
    source_ids = jnp.arange(N_EXPERT, dtype=jnp.int32)[:, None, None]

    def one_group(summed, pieces):
        group_tokens, group_grads, group_combine, group_routes = pieces
        slot_index = jax.vmap(lambda one: route_slots(one, N_EXPERT))(group_routes)
        position = (source_ids * CAP + slot_index).astype(jnp.int32)
        scaled = (group_combine[:, :, :, None] * group_grads[:, :, None, :].astype(jnp.float32)).astype(jnp.bfloat16)
        spread_inputs = jnp.broadcast_to(group_tokens[:, :, None, :], (N_EXPERT, TOK_DEV, TOP, D))
        buffer_inputs = jnp.zeros((N_EXPERT, N_EXPERT * CAP, D), jnp.bfloat16).at[group_routes, position].set(spread_inputs)
        buffer_grads = jnp.zeros((N_EXPERT, N_EXPERT * CAP, D), jnp.bfloat16).at[group_routes, position].set(scaled)

        def one_expert(items):
            row_inputs, row_grads, one_gate_up, one_down = items
            d_rows, hidden, d_preact = row_work(row_inputs, row_grads, one_gate_up, one_down)
            partial_value = expert_grads(row_inputs, row_grads, hidden, d_preact).astype(jnp.bfloat16)
            return d_rows, partial_value

        d_buffer, partials = lax.map(one_expert, (buffer_inputs, buffer_grads, gate_up, down_weight))
        route_rows = d_buffer[group_routes, position]
        d_group = jnp.sum(route_rows.astype(jnp.float32), axis=2).astype(jnp.bfloat16)
        return summed + partials.astype(jnp.float32), d_group

    start = jnp.zeros((N_EXPERT, D, 3 * H), jnp.float32)
    summed, d_groups = lax.scan(one_group, start, (tok_groups, grad_groups, combine_groups, route_groups))
    d_tokens = d_groups.reshape(TOKENS, D)
    d_gate_weight = summed[:, :, :H]
    d_up_weight = summed[:, :, H:2 * H]
    d_down_weight = jnp.transpose(summed[:, :, 2 * H:], (0, 2, 1))
    return d_tokens, d_gate_weight, d_up_weight, d_down_weight
```

```python
import jax
import jax.numpy as jnp
from jax import lax
from jax.sharding import PartitionSpec as P


def route_slots(routes, experts):
    matches = (routes[:, :, None] == jnp.arange(experts, dtype=jnp.int32)[None, None, :]).astype(
        jnp.int32
    )
    per_token = jnp.sum(matches, axis=1)
    tok_count = per_token.shape[0]
    before = jnp.tri(tok_count, k=-1, dtype=jnp.bfloat16)
    earlier = jnp.dot(
        before, per_token.astype(jnp.bfloat16), preferred_element_type=jnp.float32
    ).astype(jnp.int32)
    return jnp.sum(matches * earlier[:, None, :], axis=2)


def row_work(row_inputs, row_grads, gate_up, down_matrix):
    hidden_units = down_matrix.shape[0]
    preact = jnp.dot(row_inputs, gate_up, preferred_element_type=jnp.float32)
    gate_pre = preact[:, :hidden_units]
    up_pre = preact[:, hidden_units:]
    gate_sigmoid = jax.nn.sigmoid(gate_pre)
    hidden = (gate_pre * gate_sigmoid * up_pre).astype(jnp.bfloat16)
    d_hidden = jnp.dot(row_grads, down_matrix.T, preferred_element_type=jnp.float32)
    d_gate_pre = d_hidden * up_pre * gate_sigmoid * (1.0 + gate_pre * (1.0 - gate_sigmoid))
    d_up_pre = d_hidden * gate_pre * gate_sigmoid
    d_preact = jnp.concatenate([d_gate_pre, d_up_pre], axis=1).astype(jnp.bfloat16)
    d_rows = jnp.dot(d_preact, gate_up.T, preferred_element_type=jnp.float32).astype(jnp.bfloat16)
    return (d_rows, hidden, d_preact)


def body(tokens, d_output, combine, routes, gate_weight, up_weight, down_weight):
    experts = lax.axis_size("expert")
    tok_count = tokens.shape[0]
    model_width = tokens.shape[1]
    top_count = routes.shape[1]
    capacity = max(2, (9 * tok_count * top_count + 8 * experts - 1) // (8 * experts))
    slot_count = experts * capacity
    slot_index = route_slots(routes, experts)
    position = (routes * capacity + slot_index).reshape(-1)
    spread_inputs = jnp.repeat(tokens, top_count, axis=0)
    scaled = (
        (combine[:, :, None] * d_output[:, None, :].astype(jnp.float32))
        .astype(jnp.bfloat16)
        .reshape(-1, model_width)
    )
    send_inputs = (
        jnp.zeros((slot_count, model_width), jnp.bfloat16)
        .at[position]
        .set(spread_inputs)
        .reshape(experts, capacity, model_width)
    )
    send_grads = (
        jnp.zeros((slot_count, model_width), jnp.bfloat16)
        .at[position]
        .set(scaled)
        .reshape(experts, capacity, model_width)
    )
    whole_gate, whole_up, whole_down = (
        lax.all_gather(gate_weight, "dp", axis=1, tiled=True),
        lax.all_gather(up_weight, "dp", axis=1, tiled=True),
        lax.all_gather(down_weight, "dp", axis=2, tiled=True),
    )
    gate_up = jnp.concatenate([whole_gate[0], whole_up[0]], axis=1)
    down_matrix = whole_down[0]
    hidden_units = down_matrix.shape[0]
    recv_inputs, recv_grads = (
        lax.all_to_all(send_inputs, "expert", split_axis=0, concat_axis=0, tiled=True),
        lax.all_to_all(send_grads, "expert", split_axis=0, concat_axis=0, tiled=True),
    )
    flat_inputs = recv_inputs.reshape(-1, model_width)
    flat_grads = recv_grads.reshape(-1, model_width)
    d_rows, hidden, d_preact = row_work(flat_inputs, flat_grads, gate_up, down_matrix)
    returned = lax.all_to_all(
        d_rows.reshape(experts, capacity, model_width),
        "expert",
        split_axis=0,
        concat_axis=0,
        tiled=True,
    )
    route_rows = returned.reshape(-1, model_width)[position].reshape(
        tok_count, top_count, model_width
    )
    d_tokens = jnp.sum(route_rows.astype(jnp.float32), axis=1).astype(jnp.bfloat16)
    gate_up_grad = jnp.dot(flat_inputs.T, d_preact, preferred_element_type=jnp.float32)
    down_grad = jnp.dot(flat_grads.T, hidden, preferred_element_type=jnp.float32)
    stacked = jnp.concatenate([gate_up_grad, down_grad], axis=1)
    summed = lax.psum_scatter(
        stacked.astype(jnp.bfloat16), "dp", scatter_dimension=0, tiled=True
    ).astype(jnp.float32)
    d_gate_weight = summed[:, :hidden_units][None]
    d_up_weight = summed[:, hidden_units : 2 * hidden_units][None]
    d_down_weight = summed[:, 2 * hidden_units :].T[None]
    return (d_tokens, d_gate_weight, d_up_weight, d_down_weight)


def solution(mesh):
    placed = (
        P(("dp", "expert"), None),
        P(("dp", "expert"), None),
        P(("dp", "expert"), None),
        P(("dp", "expert"), None),
        P("expert", "dp", None),
        P("expert", "dp", None),
        P("expert", None, "dp"),
    )
    return jax.shard_map(
        body,
        mesh=mesh,
        in_specs=placed,
        out_specs=(
            P(("dp", "expert"), None),
            P("expert", "dp", None),
            P("expert", "dp", None),
            P("expert", None, "dp"),
        ),
        check_vma=False,
    )
```

```python
import jax
import jax.numpy as jnp
from jax import lax
from jax.sharding import PartitionSpec as P


def slot_map(routes, combine, experts, capacity):
    tok_count = routes.shape[0]
    ids = jnp.arange(experts, dtype=jnp.int32)[:, None, None]
    matches = routes.T[None, :, :] == ids
    member = jnp.any(matches, axis=1)
    scale = jnp.sum(jnp.where(matches, combine.T[None], 0.0), axis=1)
    before = jnp.triu(jnp.ones((tok_count, tok_count), jnp.bfloat16), k=1)
    rank = jnp.dot(
        member.astype(jnp.bfloat16), before, preferred_element_type=jnp.float32
    ).astype(jnp.int32)
    slots = jnp.arange(capacity, dtype=jnp.int32)[None, :, None]
    pick = (rank[:, None, :] == slots) & member[:, None, :]
    slot_scale = jnp.sum(jnp.where(pick, scale[:, None, :], 0.0), axis=2)
    return pick.astype(jnp.bfloat16), slot_scale


def row_work(row_inputs, row_grads, gate_up, down_t):
    hidden_units = down_t.shape[1]
    preact = jnp.dot(row_inputs, gate_up, preferred_element_type=jnp.float32)
    gate_pre = preact[:, :hidden_units]
    up_pre = preact[:, hidden_units:]
    gate_sigmoid = jax.nn.sigmoid(gate_pre)
    hidden = (gate_pre * gate_sigmoid * up_pre).astype(jnp.bfloat16)
    d_hidden = jnp.dot(row_grads, down_t, preferred_element_type=jnp.float32)
    d_gate_pre = d_hidden * up_pre * gate_sigmoid * (1.0 + gate_pre * (1.0 - gate_sigmoid))
    d_up_pre = d_hidden * gate_pre * gate_sigmoid
    d_preact = jnp.concatenate([d_gate_pre, d_up_pre], axis=1).astype(jnp.bfloat16)
    d_rows = jnp.dot(d_preact, gate_up.T, preferred_element_type=jnp.float32).astype(jnp.bfloat16)
    return (d_rows, hidden, d_preact)


def body(tokens, d_output, combine, routes, gate_weight, up_weight, down_weight):
    experts = lax.axis_size("expert")
    tok_count = tokens.shape[0]
    model_width = tokens.shape[1]
    hidden_units = gate_weight.shape[2]
    top_count = routes.shape[1]
    capacity = max(2, (9 * tok_count * top_count + 8 * experts - 1) // (8 * experts))
    mine = jnp.concatenate([gate_weight[0], up_weight[0], down_weight[0].T], axis=1)
    whole = lax.all_gather(mine, "dp", axis=0, tiled=True)
    pick, slot_scale = slot_map(routes, combine, experts, capacity)
    send_inputs = jnp.einsum(
        "ect,td->ecd", pick, tokens, preferred_element_type=jnp.float32
    ).astype(jnp.bfloat16)
    send_grads = (
        slot_scale[:, :, None]
        * jnp.einsum("ect,td->ecd", pick, d_output, preferred_element_type=jnp.float32)
    ).astype(jnp.bfloat16)
    recv_inputs, recv_grads = (
        lax.all_to_all(send_inputs, "expert", split_axis=0, concat_axis=0, tiled=True),
        lax.all_to_all(send_grads, "expert", split_axis=0, concat_axis=0, tiled=True),
    )
    flat_inputs = recv_inputs.reshape(-1, model_width)
    flat_grads = recv_grads.reshape(-1, model_width)
    gate_up = whole[:, : 2 * hidden_units]
    down_t = whole[:, 2 * hidden_units :]
    d_rows, hidden, d_preact = row_work(flat_inputs, flat_grads, gate_up, down_t)
    returned = lax.all_to_all(
        d_rows.reshape(experts, capacity, model_width),
        "expert",
        split_axis=0,
        concat_axis=0,
        tiled=True,
    )
    d_tokens = jnp.einsum(
        "ect,ecd->td", pick, returned, preferred_element_type=jnp.float32
    ).astype(jnp.bfloat16)
    gate_up_grad = jnp.dot(flat_inputs.T, d_preact, preferred_element_type=jnp.float32)
    down_grad = jnp.dot(flat_grads.T, hidden, preferred_element_type=jnp.float32)
    stacked = jnp.concatenate([gate_up_grad, down_grad], axis=1)
    summed = lax.psum_scatter(
        stacked.astype(jnp.bfloat16), "dp", scatter_dimension=0, tiled=True
    ).astype(jnp.float32)
    d_gate_weight = summed[:, :hidden_units][None]
    d_up_weight = summed[:, hidden_units : 2 * hidden_units][None]
    d_down_weight = summed[:, 2 * hidden_units :].T[None]
    return (d_tokens, d_gate_weight, d_up_weight, d_down_weight)


def solution(mesh):
    placed = (
        P(("dp", "expert"), None),
        P(("dp", "expert"), None),
        P(("dp", "expert"), None),
        P(("dp", "expert"), None),
        P("expert", "dp", None),
        P("expert", "dp", None),
        P("expert", None, "dp"),
    )
    return jax.shard_map(
        body,
        mesh=mesh,
        in_specs=placed,
        out_specs=(
            P(("dp", "expert"), None),
            P("expert", "dp", None),
            P("expert", "dp", None),
            P("expert", None, "dp"),
        ),
        check_vma=False,
    )
```

```python
import functools

import jax
import jax.numpy as jnp
from jax import lax
from jax.experimental import pallas as pl
from jax.experimental.pallas import tpu as pltpu
from jax.sharding import PartitionSpec as P

MESH = pl.DeviceIdType.MESH
F32 = jnp.float32
BF16 = jnp.bfloat16

NX, NY, NC, NZ = 4, 8, 2, 8
BLOCKS = 32
FULL = 16
CAP = 18
STEPS = ((4, 3), (3, 4))


def iota(shape, dim):
    return lax.broadcasted_iota(jnp.int32, shape, dim)


def y_shift(j, core):
    return j + 4 * (j // 3) + 4 * core * ((j // 2) % 2) * ((j + 1) % 2)


def far_first(k):
    return (2 + k) * (1 - k // 2) + (3 - k) * (k // 2)


def block_at(i):
    dx = far_first(i // 8)
    j = far_first((i // 2) % 4)
    return (dx * 4 + j) * 2 + i % 2


def dot_tn(a, b):
    return lax.dot_general(a, b, (((0,), (0,)), ((), ())), preferred_element_type=F32)


def dot_nt(a, b):
    return lax.dot_general(a, b, (((1,), (1,)), ((), ())), preferred_element_type=F32)


def kernel(
    tok,
    dout,
    comb,
    rout,
    gate,
    up,
    down,
    o_tok,
    o_gate,
    o_up,
    o_down,
    rank,
    scale,
    pick_lo,
    pick_hi,
    pick_left,
    w,
    sx,
    sg,
    rx,
    rg,
    xe,
    ge,
    dr,
    dph,
    sr,
    rr,
    wg,
    part,
    swap,
    swap_in,
    sem_xs,
    sem_xr,
    sem_gs,
    sem_gr,
    sem_rs,
    sem_rr,
    ag_s,
    ag_r,
    red_s,
    red_r,
    sw_s,
    sw_r,
):
    z = lax.axis_index("dp")
    e = lax.axis_index("expert")
    x, y, c = e // 16, (e // 2) % 8, e % 2
    b_own = y // 4
    b_oth = 1 - b_own
    n_tok, width = tok.shape
    hid = gate.shape[2]
    shard = width // NZ
    left = 2 * width
    quarter = width // 4
    rows_main = BLOCKS * FULL
    rows_all = BLOCKS * CAP
    partner = (z, x * 16 + ((y + 4) % 8) * 2 + c)

    def target(o):
        dx, j, dc = o // 8, (o // 2) % 4, o % 2
        return (x + dx) % 4, (y + y_shift(j, c)) % 8, (c + dc) % 2

    def forward(o):
        xd, yd, cd = target(o)
        return (z, xd * 16 + yd * 2 + cd)

    def backward(o):
        dx, j, dc = o // 8, (o // 2) % 4, o % 2
        cs = (c + dc) % 2
        return (z, ((x + 4 - dx) % 4) * 16 + ((y + 8 - y_shift(j, cs)) % 8) * 2 + cs)

    def z_next(d):
        return ((z + (1 if d == 0 else NZ - 1)) % NZ, e)

    barrier = pltpu.get_barrier_semaphore()

    @pl.loop(1, BLOCKS)
    def _(o):
        pl.semaphore_signal(barrier, inc=1, device_id=forward(o), device_id_type=MESH)
        pl.semaphore_signal(barrier, inc=1, device_id=backward(o), device_id_type=MESH)

    for d in range(2):
        pl.semaphore_signal(barrier, inc=1, device_id=z_next(d), device_id_type=MESH)
    pl.semaphore_signal(barrier, inc=1, device_id=partner, device_id_type=MESH)

    def slice_at(k):
        return pl.ds(pl.multiple_of(((z + k + 2 * NZ) % NZ) * shard, shard), shard)

    w[b_own, slice_at(0), :hid] = gate[0]
    w[b_own, slice_at(0), hid : 2 * hid] = up[0]
    w[b_own, slice_at(0), 2 * hid :] = down[0].T

    experts = NX * NY * NC
    ids = iota((experts, n_tok), 0)
    routes_t = rout[...].T
    comb_t = comb[...].T
    member = jnp.zeros((experts, n_tok), jnp.bool_)
    weight = jnp.zeros((experts, n_tok), F32)
    for k in range(rout.shape[1]):
        hit = routes_t[k : k + 1, :] == ids
        member = member | hit
        weight = weight + jnp.where(hit, comb_t[k : k + 1, :], 0.0)
    before = jnp.where(iota((n_tok, n_tok), 0) < iota((n_tok, n_tok), 1), 1.0, 0.0)
    count = jnp.dot(
        jnp.where(member, 1.0, 0.0).astype(BF16), before.astype(BF16), preferred_element_type=F32
    )
    rank[...] = jnp.where(member, count, -1.0)
    scale[...] = weight

    pl.semaphore_wait(barrier, 2 * (BLOCKS - 1) + 3)

    def swap_weights():
        return pltpu.make_async_remote_copy(
            src_ref=w.at[b_own, slice_at(0)],
            dst_ref=w.at[b_own, slice_at(0)],
            send_sem=sw_s.at[0],
            recv_sem=sw_r.at[0],
            device_id=partner,
            device_id_type=MESH,
        )

    def swap_weights_in():
        return pltpu.make_async_remote_copy(
            src_ref=w.at[b_oth, slice_at(0)],
            dst_ref=w.at[b_oth, slice_at(0)],
            send_sem=sw_s.at[0],
            recv_sem=sw_r.at[0],
            device_id=partner,
            device_id_type=MESH,
        )

    def gather_step(who, d, s, arriving=False):
        b = (b_own, b_oth)[who]
        sign = 1 if d == 0 else -1
        at = slice_at(-sign * (s + (1 if arriving else 0)))
        return pltpu.make_async_remote_copy(
            src_ref=w.at[b, at],
            dst_ref=w.at[b, at],
            send_sem=ag_s.at[who, d, s],
            recv_sem=ag_r.at[who, d, s],
            device_id=z_next(d),
            device_id_type=MESH,
        )

    swap_weights().start()
    for d in range(2):
        gather_step(0, d, 0).start()

    row = iota((3 * FULL, n_tok), 0)
    left_row = row % FULL
    is_hi = ((row // FULL) == 1) | (((row // FULL) == 2) & ((left_row % 4) >= 2))
    slot = jnp.where(row // FULL == 2, FULL + row % 2, row % FULL).astype(F32)
    q_row = iota((FULL, quarter), 0) // 4

    def pick_of(o):
        xd, yd, cd = target(o)
        lo = xd * 16 + (yd % 4) * 2 + cd
        chosen = jnp.where(is_hi, rank[pl.ds(lo + 8, 1), :], rank[pl.ds(lo, 1), :])
        return lo, chosen == slot

    def store_block(dst, o, block):
        dst[o, :, :width] = block[:FULL].astype(BF16)
        dst[o, :, width:left] = block[FULL : 2 * FULL].astype(BF16)
        rest = block[2 * FULL :]
        packed = jnp.zeros((FULL, quarter), F32)
        for q in range(4):
            packed = jnp.where(q_row == q, rest[:, q * quarter : (q + 1) * quarter], packed)
        dst[o, :, left:] = packed.astype(BF16)

    def send_block(src, dst, o, s_sem, r_sem, to):
        pltpu.make_async_remote_copy(
            src_ref=src.at[o],
            dst_ref=dst.at[o],
            send_sem=s_sem,
            recv_sem=r_sem,
            device_id=to,
            device_id_type=MESH,
        ).start()

    def whole(src, dst, s_sem, r_sem):
        return pltpu.make_async_remote_copy(
            src_ref=src.at[pl.ds(1, BLOCKS - 1)],
            dst_ref=dst.at[pl.ds(1, BLOCKS - 1)],
            send_sem=s_sem,
            recv_sem=r_sem,
            device_id=partner,
            device_id_type=MESH,
        )

    group = 4

    @pl.loop(0, BLOCKS // group)
    def _(i):
        picks = []
        for u in range(group):
            o = block_at(i * group + u)
            _, hit = pick_of(o)
            one_hot = jnp.where(hit, 1.0, 0.0).astype(BF16)
            pick_lo[o] = one_hot[:FULL]
            pick_hi[o] = one_hot[FULL : 2 * FULL]
            pick_left[o] = one_hot[2 * FULL :]
            picks.append(one_hot)
        block = jnp.dot(jnp.concatenate(picks, axis=0), tok[...], preferred_element_type=F32)
        for u in range(group):
            o = block_at(i * group + u)
            store_block(sx, o, block[u * 3 * FULL : (u + 1) * 3 * FULL])

            @pl.when(i * group + u < BLOCKS - 2)
            def _():
                send_block(sx, rx, o, sem_xs, sem_xr, forward(o))

    send_block(sx, rx, 1, sem_xs, sem_xr, forward(1))
    rx[0] = sx[0]
    swap_weights_in().wait_recv()
    for d in range(2):
        gather_step(1, d, 0).start()

    @pl.loop(0, BLOCKS // group)
    def _(i):
        picks, scales = [], []
        for u in range(group):
            o = block_at(i * group + u)
            lo, hit = pick_of(o)
            chosen = jnp.where(is_hi, scale[pl.ds(lo + 8, 1), :], scale[pl.ds(lo, 1), :])
            scales.append(jnp.sum(jnp.where(hit, chosen, 0.0), axis=1, keepdims=True))
            picks.append(jnp.where(hit, 1.0, 0.0).astype(BF16))
        block = jnp.dot(jnp.concatenate(picks, axis=0), dout[...], preferred_element_type=F32)
        block = block * jnp.concatenate(scales, axis=0)
        for u in range(group):
            o = block_at(i * group + u)
            store_block(sg, o, block[u * 3 * FULL : (u + 1) * 3 * FULL])

            @pl.when(i * group + u < BLOCKS - 2)
            def _():
                send_block(sg, rg, o, sem_gs, sem_gr, forward(o))

    send_block(sg, rg, 1, sem_gs, sem_gr, forward(1))
    rg[0] = sg[0]

    for s in range(1, 4):
        for who in range(2):
            for d in range(2):
                if s < STEPS[who][d]:
                    gather_step(who, d, s - 1, True).wait_recv()
                    gather_step(who, d, s).start()

    def unpack(src, dst):
        for b in range(2):
            dst[b, :rows_main, :] = src[:, :, b * width : (b + 1) * width].reshape(
                rows_main, width
            )
        rest = src[:, :, left:].reshape(rows_main, quarter)
        r = iota((4 * BLOCKS, rows_main), 0)
        base = ((r % (2 * BLOCKS)) // 2) * FULL + (r // (2 * BLOCKS)) * 2 + r % 2
        for q in range(4):
            take = jnp.where(iota((4 * BLOCKS, rows_main), 1) == base + 4 * q, 1.0, 0.0)
            part_q = jnp.dot(take.astype(BF16), rest, preferred_element_type=F32).astype(BF16)
            for b in range(2):
                dst[b, rows_main:, q * quarter : (q + 1) * quarter] = part_q[
                    b * 2 * BLOCKS : (b + 1) * 2 * BLOCKS
                ]

    whole(sx, rx, sem_xs, sem_xr).wait_recv()
    unpack(rx, xe)
    whole(sg, rg, sem_gs, sem_gr).wait_recv()
    unpack(rg, ge)
    for who in range(2):
        for d in range(2):
            gather_step(who, d, STEPS[who][d] - 1, True).wait_recv()

    chunk = 192

    def rows_of(b):
        @pl.loop(0, rows_all // chunk)
        def _(i):
            at = pl.ds(pl.multiple_of(i * chunk, chunk), chunk)
            pre = jnp.dot(xe[b, at, :], w[b, :, : 2 * hid], preferred_element_type=F32)
            d_hidden = jnp.dot(ge[b, at, :], w[b, :, 2 * hid :], preferred_element_type=F32)
            gate_pre, up_pre = pre[:, :hid], pre[:, hid:]
            sig = jax.nn.sigmoid(gate_pre)
            silu = gate_pre * sig
            d_gate = d_hidden * up_pre * sig * (1.0 + gate_pre * (1.0 - sig))
            dph[at, :hid] = d_gate.astype(BF16)
            dph[at, hid : 2 * hid] = (d_hidden * silu).astype(BF16)
            dph[at, 2 * hid :] = (silu * up_pre).astype(BF16)
            dr[b, at, :] = dot_nt(dph[at, : 2 * hid], w[b, :, : 2 * hid]).astype(BF16)

    def grads_of(b):
        for k in range(3):
            src = xe if k < 2 else ge
            total = dot_tn(dph[:, k * hid : (k + 1) * hid], src[b]).astype(BF16)
            for s in range(NZ):
                wg[b, s, k * hid : (k + 1) * hid, :] = total[:, s * shard : (s + 1) * shard]

    def red_step(who, d, s):
        b = (b_own, b_oth)[who]
        sign = 1 if d == 0 else -1
        k = STEPS[who][d] - s
        return pltpu.make_async_remote_copy(
            src_ref=wg.at[b, (z + sign * k + NZ) % NZ],
            dst_ref=part.at[who, d, s],
            send_sem=red_s.at[who, d, s],
            recv_sem=red_r.at[who, d, s],
            device_id=z_next(d),
            device_id_type=MESH,
        )

    rows_of(b_oth)
    grads_of(b_oth)
    for d in range(2):
        red_step(1, d, 0).start()
    rows_of(b_own)

    for b in range(2):
        sr[:, :, b * width : (b + 1) * width] = dr[b, :rows_main, :].reshape(BLOCKS, FULL, width)
    spread_row = iota((rows_main, 4 * BLOCKS), 0)
    spread = jnp.where(
        iota((rows_main, 4 * BLOCKS), 1)
        == ((spread_row // 2) % 2) * 2 * BLOCKS + (spread_row // FULL) * 2 + spread_row % 2,
        1.0,
        0.0,
    ).astype(BF16)
    tails = jnp.concatenate([dr[0, rows_main:, :], dr[1, rows_main:, :]], axis=0)
    tails = jnp.dot(spread, tails, preferred_element_type=F32)
    q_all = (iota((rows_main, quarter), 0) // 4) % 4
    packed = jnp.zeros((rows_main, quarter), F32)
    for q in range(4):
        packed = jnp.where(q_all == q, tails[:, q * quarter : (q + 1) * quarter], packed)
    sr[:, :, left:] = packed.astype(BF16).reshape(BLOCKS, FULL, quarter)

    @pl.loop(0, BLOCKS - 2)
    def _(i):
        o = block_at(i)
        send_block(sr, rr, o, sem_rs, sem_rr, backward(o))

    send_block(sr, rr, 1, sem_rs, sem_rr, backward(1))
    rr[0] = sr[0]

    grads_of(b_own)
    for d in range(2):
        red_step(0, d, 0).start()

    for s in range(1, 4):
        for who in (1, 0):
            for d in range(2):
                if s < STEPS[who][d]:
                    b = (b_own, b_oth)[who]
                    sign = 1 if d == 0 else -1
                    k = STEPS[who][d] - s
                    at = (z + sign * k + NZ) % NZ
                    red_step(who, d, s - 1).wait_recv()
                    wg[b, at] = (
                        wg[b, at].astype(F32) + part[who, d, s - 1].astype(F32)
                    ).astype(BF16)
                    red_step(who, d, s).start()

    def final(who):
        b = (b_own, b_oth)[who]
        total = wg[b, z].astype(F32)
        for d in range(2):
            last = STEPS[who][d] - 1
            red_step(who, d, last).wait_recv()
            total = total + part[who, d, last].astype(F32)
        return total

    swap[...] = final(1).astype(BF16)
    swap_grads = pltpu.make_async_remote_copy(
        src_ref=swap,
        dst_ref=swap_in,
        send_sem=sw_s.at[1],
        recv_sem=sw_r.at[1],
        device_id=partner,
        device_id_type=MESH,
    )
    swap_grads.start()

    whole(sr, rr, sem_rs, sem_rr).wait_recv()
    d_tok = dot_tn(
        pick_lo[...].reshape(rows_main, n_tok), rr[:, :, :width].reshape(rows_main, width)
    ) + dot_tn(
        pick_hi[...].reshape(rows_main, n_tok), rr[:, :, width:left].reshape(rows_main, width)
    )
    tail_pick = pick_left[...].reshape(rows_main, n_tok)
    tail = rr[:, :, left:].reshape(rows_main, quarter)
    q_pick = (iota((rows_main, n_tok), 0) // 4) % 4
    for q in range(4):
        one = jnp.where(q_pick == q, tail_pick.astype(F32), 0.0).astype(BF16)
        o_tok[:, q * quarter : (q + 1) * quarter] = (
            d_tok[:, q * quarter : (q + 1) * quarter] + dot_tn(one, tail)
        ).astype(BF16)

    total = final(0)
    swap_grads.wait_recv()
    total = total + swap_in[...].astype(F32)
    o_gate[0] = total[:hid].T
    o_up[0] = total[hid : 2 * hid].T
    o_down[0] = total[2 * hid :]

    whole(sx, rx, sem_xs, sem_xr).wait_send()
    whole(sg, rg, sem_gs, sem_gr).wait_send()
    whole(sr, rr, sem_rs, sem_rr).wait_send()
    swap_weights().wait_send()
    swap_grads.wait_send()
    for who in range(2):
        for d in range(2):
            for s in range(STEPS[who][d]):
                gather_step(who, d, s).wait_send()
                red_step(who, d, s).wait_send()


def body(tokens, d_output, combine, routes, gate_weight, up_weight, down_weight):
    n_tok, width = tokens.shape
    hid = gate_weight.shape[2]
    shard = width // NZ
    block = (BLOCKS, FULL, 2 * width + width // 4)
    rows = BLOCKS * CAP
    vmem = pl.BlockSpec(memory_space=pltpu.VMEM)
    dma = pltpu.SemaphoreType.DMA
    return pl.pallas_call(
        kernel,
        out_shape=(
            jax.ShapeDtypeStruct((n_tok, width), BF16),
            jax.ShapeDtypeStruct((1, shard, hid), F32),
            jax.ShapeDtypeStruct((1, shard, hid), F32),
            jax.ShapeDtypeStruct((1, hid, shard), F32),
        ),
        in_specs=[vmem] * 7,
        out_specs=(vmem,) * 4,
        scratch_shapes=[
            pltpu.VMEM((NX * NY * NC, n_tok), F32),
            pltpu.VMEM((NX * NY * NC, n_tok), F32),
            pltpu.VMEM((BLOCKS, FULL, n_tok), BF16),
            pltpu.VMEM((BLOCKS, FULL, n_tok), BF16),
            pltpu.VMEM((BLOCKS, FULL, n_tok), BF16),
            pltpu.VMEM((2, width, 3 * hid), BF16),
            pltpu.VMEM(block, BF16),
            pltpu.VMEM(block, BF16),
            pltpu.VMEM(block, BF16),
            pltpu.VMEM(block, BF16),
            pltpu.VMEM((2, rows, width), BF16),
            pltpu.VMEM((2, rows, width), BF16),
            pltpu.VMEM((2, rows, width), BF16),
            pltpu.VMEM((rows, 3 * hid), BF16),
            pltpu.VMEM(block, BF16),
            pltpu.VMEM(block, BF16),
            pltpu.VMEM((2, NZ, 3 * hid, shard), BF16),
            pltpu.VMEM((2, 2, 4, 3 * hid, shard), BF16),
            pltpu.VMEM((3 * hid, shard), BF16),
            pltpu.VMEM((3 * hid, shard), BF16),
            dma,
            dma,
            dma,
            dma,
            dma,
            dma,
            dma((2, 2, 4)),
            dma((2, 2, 4)),
            dma((2, 2, 4)),
            dma((2, 2, 4)),
            dma((2,)),
            dma((2,)),
        ],
        compiler_params=pltpu.CompilerParams(
            collective_id=0, has_side_effects=True, vmem_limit_bytes=56 << 20
        ),
        name="moe_backward",
    )(tokens, d_output, combine, routes, gate_weight, up_weight, down_weight)


def solution(mesh):
    placed = (
        P(("dp", "expert"), None),
        P(("dp", "expert"), None),
        P(("dp", "expert"), None),
        P(("dp", "expert"), None),
        P("expert", "dp", None),
        P("expert", "dp", None),
        P("expert", None, "dp"),
    )
    return jax.shard_map(
        body,
        mesh=mesh,
        in_specs=placed,
        out_specs=(
            P(("dp", "expert"), None),
            P("expert", "dp", None),
            P("expert", "dp", None),
            P("expert", None, "dp"),
        ),
        check_vma=False,
    )
```

```python
import functools

import jax
import jax.numpy as jnp
from jax import lax
from jax.experimental import pallas as pl
from jax.experimental.pallas import tpu as pltpu
from jax.sharding import PartitionSpec as P

MESH = pl.DeviceIdType.MESH
F32 = jnp.float32
BF16 = jnp.bfloat16

NX, NY, NC, NZ = 4, 8, 2, 8
BLOCKS = 32
FULL = 16
CAP = 18
SELF = 3
STEPS = ((4, 3), (3, 4))


def iota(shape, dim):
    return lax.broadcasted_iota(jnp.int32, shape, dim)


def y_shift(j, core):
    return j + 4 * (j // 3) + 4 * core * ((j // 2) % 2) * ((j + 1) % 2)


def far_first(k):
    return (2 + k) * (1 - k // 2) + (3 - k) * (k // 2)


def block_at(i):
    dx = far_first(i % 4)
    j = (dx + 4 - (i // 4) % 4) % 4
    return (dx * 4 + j) * 2 + i // 16


def dot_tn(a, b):
    return lax.dot_general(a, b, (((0,), (0,)), ((), ())), preferred_element_type=F32)


def dot_nt(a, b):
    return lax.dot_general(a, b, (((1,), (1,)), ((), ())), preferred_element_type=F32)


def kernel(
    tok,
    dout,
    comb,
    rout,
    gate,
    up,
    down,
    o_tok,
    o_gate,
    o_up,
    o_down,
    rank,
    scale,
    pick_lo,
    pick_hi,
    pick_left,
    w,
    sx,
    sg,
    rx,
    rg,
    xe,
    ge,
    dr,
    pre,
    dph,
    sr,
    rr,
    wg,
    part,
    swap,
    swap_in,
    sem_xs,
    sem_xr,
    sem_gs,
    sem_gr,
    sem_rs,
    sem_rr,
    ag_s,
    ag_r,
    red_s,
    red_r,
    sw_s,
    sw_r,
):
    z = lax.axis_index("dp")
    e = lax.axis_index("expert")
    x, y, c = e // 16, (e // 2) % 8, e % 2
    b_own = y // 4
    b_oth = 1 - b_own
    n_tok, width = tok.shape
    hid = gate.shape[2]
    shard = width // NZ
    left = 2 * width
    quarter = width // 4
    rows_main = BLOCKS * FULL
    rows_all = BLOCKS * CAP
    partner = (z, x * 16 + ((y + 4) % 8) * 2 + c)

    def target(o):
        dx, j, dc = o // 8, (o // 2) % 4, o % 2
        return (x + dx) % 4, (y + y_shift(j, c)) % 8, (c + dc) % 2

    def forward(o):
        xd, yd, cd = target(o)
        return (z, xd * 16 + yd * 2 + cd)

    def backward(o):
        dx, j, dc = o // 8, (o // 2) % 4, o % 2
        cs = (c + dc) % 2
        return (z, ((x + 4 - dx) % 4) * 16 + ((y + 8 - y_shift(j, cs)) % 8) * 2 + cs)

    def z_next(d):
        return ((z + (1 if d == 0 else NZ - 1)) % NZ, e)

    barrier = pltpu.get_barrier_semaphore()

    @pl.loop(1, BLOCKS)
    def _(o):
        pl.semaphore_signal(barrier, inc=1, device_id=forward(o), device_id_type=MESH)
        pl.semaphore_signal(barrier, inc=1, device_id=backward(o), device_id_type=MESH)

    for d in range(2):
        pl.semaphore_signal(barrier, inc=1, device_id=z_next(d), device_id_type=MESH)
    pl.semaphore_signal(barrier, inc=1, device_id=partner, device_id_type=MESH)

    def slice_at(k):
        return pl.ds(pl.multiple_of(((z + k + 2 * NZ) % NZ) * shard, shard), shard)

    w[b_own, slice_at(0), :hid] = gate[0]
    w[b_own, slice_at(0), hid : 2 * hid] = up[0]
    w[b_own, slice_at(0), 2 * hid :] = down[0].T

    experts = NX * NY * NC
    ids = iota((experts, n_tok), 0)
    routes_t, comb_t = rout[...], comb[...]
    member = jnp.zeros((experts, n_tok), jnp.bool_)
    weight = jnp.zeros((experts, n_tok), F32)
    for k in range(rout.shape[0]):
        hit = routes_t[k : k + 1, :] == ids
        member = member | hit
        weight = weight + jnp.where(hit, comb_t[k : k + 1, :], 0.0)
    before = jnp.where(iota((n_tok, n_tok), 0) < iota((n_tok, n_tok), 1), 1.0, 0.0)
    count = jnp.dot(
        jnp.where(member, 1.0, 0.0).astype(BF16), before.astype(BF16), preferred_element_type=F32
    )
    rank[...] = jnp.where(member, count, -1.0)
    scale[...] = weight

    pl.semaphore_wait(barrier, 2 * (BLOCKS - 1) + 3)

    def swap_weights():
        return pltpu.make_async_remote_copy(
            src_ref=w.at[b_own, slice_at(0)],
            dst_ref=w.at[b_own, slice_at(0)],
            send_sem=sw_s.at[0],
            recv_sem=sw_r.at[0],
            device_id=partner,
            device_id_type=MESH,
        )

    def swap_weights_in():
        return pltpu.make_async_remote_copy(
            src_ref=w.at[b_oth, slice_at(0)],
            dst_ref=w.at[b_oth, slice_at(0)],
            send_sem=sw_s.at[0],
            recv_sem=sw_r.at[0],
            device_id=partner,
            device_id_type=MESH,
        )

    def gather_step(who, d, s, arriving=False):
        b = (b_own, b_oth)[who]
        sign = 1 if d == 0 else -1
        at = slice_at(-sign * (s + (1 if arriving else 0)))
        return pltpu.make_async_remote_copy(
            src_ref=w.at[b, at],
            dst_ref=w.at[b, at],
            send_sem=ag_s.at[who, d, s],
            recv_sem=ag_r.at[who, d, s],
            device_id=z_next(d),
            device_id_type=MESH,
        )

    def gather_next(who, s):
        for d in range(2):
            if s < STEPS[who][d]:
                gather_step(who, d, s - 1, True).wait_recv()
                gather_step(who, d, s).start()

    swap_weights().start()
    for d in range(2):
        gather_step(0, d, 0).start()

    row = iota((3 * FULL, n_tok), 0)
    left_row = row % FULL
    is_hi = ((row // FULL) == 1) | (((row // FULL) == 2) & ((left_row % 4) >= 2))
    slot = jnp.where(row // FULL == 2, FULL + row % 2, row % FULL).astype(F32)
    q_row = iota((FULL, quarter), 0) // 4

    def pick_of(o):
        xd, yd, cd = target(o)
        lo = xd * 16 + (yd % 4) * 2 + cd
        chosen = jnp.where(is_hi, rank[pl.ds(lo + 8, 1), :], rank[pl.ds(lo, 1), :])
        return lo, chosen == slot

    def store_block(dst, o, block):
        dst[o, :, :width] = block[:FULL].astype(BF16)
        dst[o, :, width:left] = block[FULL : 2 * FULL].astype(BF16)
        rest = block[2 * FULL :]
        packed = jnp.zeros((FULL, quarter), F32)
        for q in range(4):
            packed = jnp.where(q_row == q, rest[:, q * quarter : (q + 1) * quarter], packed)
        dst[o, :, left:] = packed.astype(BF16)

    def send_block(src, dst, o, s_sem, r_sem, to):
        pltpu.make_async_remote_copy(
            src_ref=src.at[o],
            dst_ref=dst.at[o],
            send_sem=s_sem,
            recv_sem=r_sem,
            device_id=to,
            device_id_type=MESH,
        ).start()

    def whole(src, dst, s_sem, r_sem):
        return pltpu.make_async_remote_copy(
            src_ref=src.at[pl.ds(1, BLOCKS - 1)],
            dst_ref=dst.at[pl.ds(1, BLOCKS - 1)],
            send_sem=s_sem,
            recv_sem=r_sem,
            device_id=partner,
            device_id_type=MESH,
        )

    group = 4

    @pl.loop(0, BLOCKS // group)
    def _(i):
        picks = []
        for u in range(group):
            o = block_at(i * group + u)
            _, hit = pick_of(o)
            one_hot = jnp.where(hit, 1.0, 0.0).astype(BF16)
            pick_lo[o] = one_hot[:FULL]
            pick_hi[o] = one_hot[FULL : 2 * FULL]
            pick_left[o] = one_hot[2 * FULL :]
            picks.append(one_hot)
        block = jnp.dot(jnp.concatenate(picks, axis=0), tok[...], preferred_element_type=F32)
        for u in range(group):
            o = block_at(i * group + u)
            store_block(sx, o, block[u * 3 * FULL : (u + 1) * 3 * FULL])

            @pl.when(i * group + u != SELF)
            def _():
                send_block(sx, rx, o, sem_xs, sem_xr, forward(o))

    rx[0] = sx[0]
    gather_next(0, 1)

    @pl.loop(0, BLOCKS // group)
    def _(i):
        picks, scales = [], []
        for u in range(group):
            o = block_at(i * group + u)
            lo, hit = pick_of(o)
            chosen = jnp.where(is_hi, scale[pl.ds(lo + 8, 1), :], scale[pl.ds(lo, 1), :])
            scales.append(jnp.sum(jnp.where(hit, chosen, 0.0), axis=1, keepdims=True))
            picks.append(jnp.where(hit, 1.0, 0.0).astype(BF16))
        block = jnp.dot(jnp.concatenate(picks, axis=0), dout[...], preferred_element_type=F32)
        block = block * jnp.concatenate(scales, axis=0)
        for u in range(group):
            o = block_at(i * group + u)
            store_block(sg, o, block[u * 3 * FULL : (u + 1) * 3 * FULL])

            @pl.when(i * group + u != SELF)
            def _():
                send_block(sg, rg, o, sem_gs, sem_gr, forward(o))

    rg[0] = sg[0]

    gather_next(0, 2)
    swap_weights_in().wait_recv()
    for d in range(2):
        gather_step(1, d, 0).start()
    gather_next(0, 3)
    for s in range(1, 4):
        gather_next(1, s)

    def unpack(src, dst):
        for b in range(2):
            dst[b, :rows_main, :] = src[:, :, b * width : (b + 1) * width].reshape(
                rows_main, width
            )
        rest = src[:, :, left:].reshape(rows_main, quarter)
        r = iota((4 * BLOCKS, rows_main), 0)
        base = ((r % (2 * BLOCKS)) // 2) * FULL + (r // (2 * BLOCKS)) * 2 + r % 2
        for q in range(4):
            take = jnp.where(iota((4 * BLOCKS, rows_main), 1) == base + 4 * q, 1.0, 0.0)
            part_q = jnp.dot(take.astype(BF16), rest, preferred_element_type=F32).astype(BF16)
            for b in range(2):
                dst[b, rows_main:, q * quarter : (q + 1) * quarter] = part_q[
                    b * 2 * BLOCKS : (b + 1) * 2 * BLOCKS
                ]

    whole(sx, rx, sem_xs, sem_xr).wait_recv()
    unpack(rx, xe)
    for who in range(2):
        for d in range(2):
            gather_step(who, d, STEPS[who][d] - 1, True).wait_recv()

    chunk = 192

    def chunk_at(i):
        return pl.ds(pl.multiple_of(i * chunk, chunk), chunk)

    def forward_rows(b):
        @pl.loop(0, rows_all // chunk)
        def _(i):
            at = chunk_at(i)
            pre[b, at, :] = jnp.dot(xe[b, at, :], w[b, :, : 2 * hid], preferred_element_type=F32)

    def backward_rows(b):
        @pl.loop(0, rows_all // chunk)
        def _(i):
            at = chunk_at(i)
            d_hidden = jnp.dot(ge[b, at, :], w[b, :, 2 * hid :], preferred_element_type=F32)
            gate_pre, up_pre = pre[b, at, :hid], pre[b, at, hid:]
            sig = jax.nn.sigmoid(gate_pre)
            silu = gate_pre * sig
            d_gate = d_hidden * up_pre * sig * (1.0 + gate_pre * (1.0 - sig))
            dph[b, at, :hid] = d_gate.astype(BF16)
            dph[b, at, hid : 2 * hid] = (d_hidden * silu).astype(BF16)
            dph[b, at, 2 * hid :] = (silu * up_pre).astype(BF16)

    def input_rows(b):
        @pl.loop(0, rows_all // chunk)
        def _(i):
            at = chunk_at(i)
            dr[b, at, :] = dot_nt(dph[b, at, : 2 * hid], w[b, :, : 2 * hid]).astype(BF16)

    def grads_of(b):
        for k in range(3):
            src = xe if k < 2 else ge
            total = dot_tn(dph[b, :, k * hid : (k + 1) * hid], src[b]).astype(BF16)
            for s in range(NZ):
                wg[b, s, k * hid : (k + 1) * hid, :] = total[:, s * shard : (s + 1) * shard]

    def red_step(who, d, s):
        b = (b_own, b_oth)[who]
        sign = 1 if d == 0 else -1
        k = STEPS[who][d] - s
        return pltpu.make_async_remote_copy(
            src_ref=wg.at[b, (z + sign * k + NZ) % NZ],
            dst_ref=part.at[who, d, s],
            send_sem=red_s.at[who, d, s],
            recv_sem=red_r.at[who, d, s],
            device_id=z_next(d),
            device_id_type=MESH,
        )

    def red_next(who, s):
        b = (b_own, b_oth)[who]
        for d in range(2):
            if s < STEPS[who][d]:
                sign = 1 if d == 0 else -1
                at = (z + sign * (STEPS[who][d] - s) + NZ) % NZ
                red_step(who, d, s - 1).wait_recv()
                wg[b, at] = (
                    wg[b, at].astype(F32) + part[who, d, s - 1].astype(F32)
                ).astype(BF16)
                red_step(who, d, s).start()

    @pl.loop(0, 2)
    def _(b):
        forward_rows(b)

    whole(sg, rg, sem_gs, sem_gr).wait_recv()
    unpack(rg, ge)

    for who in (1, 0):
        b = (b_own, b_oth)[who]
        backward_rows(b)
        grads_of(b)
        if who == 0:
            red_next(1, 1)
        for d in range(2):
            red_step(who, d, 0).start()

    @pl.loop(0, 2)
    def _(b):
        input_rows(b)

    for b in range(2):
        sr[:, :, b * width : (b + 1) * width] = dr[b, :rows_main, :].reshape(BLOCKS, FULL, width)
    spread_row = iota((rows_main, 4 * BLOCKS), 0)
    spread = jnp.where(
        iota((rows_main, 4 * BLOCKS), 1)
        == ((spread_row // 2) % 2) * 2 * BLOCKS + (spread_row // FULL) * 2 + spread_row % 2,
        1.0,
        0.0,
    ).astype(BF16)
    tails = jnp.concatenate([dr[0, rows_main:, :], dr[1, rows_main:, :]], axis=0)
    tails = jnp.dot(spread, tails, preferred_element_type=F32)
    q_all = (iota((rows_main, quarter), 0) // 4) % 4
    packed = jnp.zeros((rows_main, quarter), F32)
    for q in range(4):
        packed = jnp.where(q_all == q, tails[:, q * quarter : (q + 1) * quarter], packed)
    sr[:, :, left:] = packed.astype(BF16).reshape(BLOCKS, FULL, quarter)

    @pl.loop(0, BLOCKS - 1)
    def _(i):
        o = block_at((i + SELF + 1) % BLOCKS)
        send_block(sr, rr, o, sem_rs, sem_rr, backward(o))

    rr[0] = sr[0]

    red_next(1, 2)
    red_next(0, 1)
    red_next(1, 3)
    red_next(0, 2)

    def final(who):
        b = (b_own, b_oth)[who]
        total = wg[b, z].astype(F32)
        for d in range(2):
            last = STEPS[who][d] - 1
            red_step(who, d, last).wait_recv()
            total = total + part[who, d, last].astype(F32)
        return total

    swap[...] = final(1).astype(BF16)
    swap_grads = pltpu.make_async_remote_copy(
        src_ref=swap,
        dst_ref=swap_in,
        send_sem=sw_s.at[1],
        recv_sem=sw_r.at[1],
        device_id=partner,
        device_id_type=MESH,
    )
    swap_grads.start()
    red_next(0, 3)

    whole(sr, rr, sem_rs, sem_rr).wait_recv()
    d_tok = dot_tn(
        pick_lo[...].reshape(rows_main, n_tok), rr[:, :, :width].reshape(rows_main, width)
    ) + dot_tn(
        pick_hi[...].reshape(rows_main, n_tok), rr[:, :, width:left].reshape(rows_main, width)
    )
    tail_pick = pick_left[...].reshape(rows_main, n_tok)
    tail = rr[:, :, left:].reshape(rows_main, quarter)
    q_pick = (iota((rows_main, n_tok), 0) // 4) % 4
    for q in range(4):
        one = jnp.where(q_pick == q, tail_pick.astype(F32), 0.0).astype(BF16)
        o_tok[:, q * quarter : (q + 1) * quarter] = (
            d_tok[:, q * quarter : (q + 1) * quarter] + dot_tn(one, tail)
        ).astype(BF16)

    total = final(0)
    swap_grads.wait_recv()
    total = total + swap_in[...].astype(F32)
    o_gate[0] = total[:hid].T
    o_up[0] = total[hid : 2 * hid].T
    o_down[0] = total[2 * hid :]

    whole(sx, rx, sem_xs, sem_xr).wait_send()
    whole(sg, rg, sem_gs, sem_gr).wait_send()
    whole(sr, rr, sem_rs, sem_rr).wait_send()
    swap_weights().wait_send()
    swap_grads.wait_send()
    for who in range(2):
        for d in range(2):
            for s in range(STEPS[who][d]):
                gather_step(who, d, s).wait_send()
                red_step(who, d, s).wait_send()


def body(tokens, d_output, combine, routes, gate_weight, up_weight, down_weight):
    n_tok, width = tokens.shape
    hid = gate_weight.shape[2]
    shard = width // NZ
    block = (BLOCKS, FULL, 2 * width + width // 4)
    rows = BLOCKS * CAP
    vmem = pl.BlockSpec(memory_space=pltpu.VMEM)
    dma = pltpu.SemaphoreType.DMA
    return pl.pallas_call(
        kernel,
        out_shape=(
            jax.ShapeDtypeStruct((n_tok, width), BF16),
            jax.ShapeDtypeStruct((1, shard, hid), F32),
            jax.ShapeDtypeStruct((1, shard, hid), F32),
            jax.ShapeDtypeStruct((1, hid, shard), F32),
        ),
        in_specs=[vmem] * 7,
        out_specs=(vmem,) * 4,
        scratch_shapes=[
            pltpu.VMEM((NX * NY * NC, n_tok), F32),
            pltpu.VMEM((NX * NY * NC, n_tok), F32),
            pltpu.VMEM((BLOCKS, FULL, n_tok), BF16),
            pltpu.VMEM((BLOCKS, FULL, n_tok), BF16),
            pltpu.VMEM((BLOCKS, FULL, n_tok), BF16),
            pltpu.VMEM((2, width, 3 * hid), BF16),
            pltpu.VMEM(block, BF16),
            pltpu.VMEM(block, BF16),
            pltpu.VMEM(block, BF16),
            pltpu.VMEM(block, BF16),
            pltpu.VMEM((2, rows, width), BF16),
            pltpu.VMEM((2, rows, width), BF16),
            pltpu.VMEM((2, rows, width), BF16),
            pltpu.VMEM((2, rows, 2 * hid), F32),
            pltpu.VMEM((2, rows, 3 * hid), BF16),
            pltpu.VMEM(block, BF16),
            pltpu.VMEM(block, BF16),
            pltpu.VMEM((2, NZ, 3 * hid, shard), BF16),
            pltpu.VMEM((2, 2, 4, 3 * hid, shard), BF16),
            pltpu.VMEM((3 * hid, shard), BF16),
            pltpu.VMEM((3 * hid, shard), BF16),
            dma,
            dma,
            dma,
            dma,
            dma,
            dma,
            dma((2, 2, 4)),
            dma((2, 2, 4)),
            dma((2, 2, 4)),
            dma((2, 2, 4)),
            dma((2,)),
            dma((2,)),
        ],
        compiler_params=pltpu.CompilerParams(
            collective_id=0, has_side_effects=True, vmem_limit_bytes=56 << 20
        ),
        name="moe_backward",
    )(tokens, d_output, combine.T, routes.T, gate_weight, up_weight, down_weight)


def solution(mesh):
    placed = (
        P(("dp", "expert"), None),
        P(("dp", "expert"), None),
        P(("dp", "expert"), None),
        P(("dp", "expert"), None),
        P("expert", "dp", None),
        P("expert", "dp", None),
        P("expert", None, "dp"),
    )
    return jax.shard_map(
        body,
        mesh=mesh,
        in_specs=placed,
        out_specs=(
            P(("dp", "expert"), None),
            P("expert", "dp", None),
            P("expert", "dp", None),
            P("expert", None, "dp"),
        ),
        check_vma=False,
    )
```

```python
import functools

import jax
import jax.numpy as jnp
from jax import lax
from jax.experimental import pallas as pl
from jax.experimental.pallas import tpu as pltpu
from jax.sharding import PartitionSpec as P

MESH = pl.DeviceIdType.MESH
F32 = jnp.float32
BF16 = jnp.bfloat16

NX, NY, NC, NZ = 4, 8, 2, 8
BLOCKS = 32
FULL = 16
CAP = 18
SELF = 3
NEAR = 4
Y_ORDER = (1, 3, 2)
X_ORDER = (2, 1, 3, 0)
STEPS = 4


def iota(shape, dim):
    return lax.broadcasted_iota(jnp.int32, shape, dim)


def y_shift(j, core):
    return j + 4 * (j // 3) + 4 * core * ((j // 2) % 2) * ((j + 1) % 2)


def far_first(k):
    return (2 + k) * (1 - k // 2) + (3 - k) * (k // 2)


def block_at(i):
    dx = far_first(i % 4)
    j = (dx + 4 - (i // 4) % 4) % 4
    return (dx * 2 + i // 16) * 4 + j


def dot_tn(a, b):
    return lax.dot_general(a, b, (((0,), (0,)), ((), ())), preferred_element_type=F32)


def dot_nt(a, b):
    return lax.dot_general(a, b, (((1,), (1,)), ((), ())), preferred_element_type=F32)


def kernel(
    tok,
    dout,
    comb,
    rout,
    gate,
    up,
    down,
    o_tok,
    o_gate,
    o_up,
    o_down,
    rank,
    scale,
    yr,
    yc,
    yx,
    yg,
    pick_lo,
    pick_hi,
    pick_left,
    w,
    sx,
    sg,
    rx,
    rg,
    xe,
    ge,
    dr,
    pre,
    dph,
    sr,
    rr,
    wg,
    part,
    swap,
    swap_in,
    sem_xs,
    sem_xr,
    sem_gs,
    sem_gr,
    sem_rs,
    sem_rr,
    sem_ys,
    sem_yr,
    ag_s,
    ag_r,
    red_s,
    red_r,
    sw_s,
    sw_r,
):
    z = lax.axis_index("dp")
    e = lax.axis_index("expert")
    x, y, c = e // 16, (e // 2) % 8, e % 2
    b_own = y // 4
    b_oth = 1 - b_own
    n_tok, width = tok.shape
    hid = gate.shape[2]
    shard = width // NZ
    left = 2 * width
    quarter = width // 4
    rows_main = BLOCKS * FULL
    rows_all = BLOCKS * CAP
    partner = (z, x * 16 + ((y + 4) % 8) * 2 + c)

    def target(o):
        dx, j, dc = o // 8, o % 4, (o // 4) % 2
        return (x + dx) % 4, (y + y_shift(j, c)) % 8, (c + dc) % 2

    def forward(o):
        xd, yd, cd = target(o)
        return (z, xd * 16 + yd * 2 + cd)

    def backward(o):
        dx, j, dc = o // 8, o % 4, (o // 4) % 2
        cs = (c + dc) % 2
        return (z, ((x + 4 - dx) % 4) * 16 + ((y + 8 - y_shift(j, cs)) % 8) * 2 + cs)

    def z_next(d):
        return ((z + (1 if d == 0 else NZ - 1)) % NZ, e)

    barrier = pltpu.get_barrier_semaphore()

    @pl.loop(1, BLOCKS)
    def _(o):
        pl.semaphore_signal(barrier, inc=1, device_id=forward(o), device_id_type=MESH)
        pl.semaphore_signal(barrier, inc=1, device_id=backward(o), device_id_type=MESH)

    for d in range(2):
        pl.semaphore_signal(barrier, inc=1, device_id=z_next(d), device_id_type=MESH)
    pl.semaphore_signal(barrier, inc=1, device_id=partner, device_id_type=MESH)

    def slice_at(k):
        return pl.ds(pl.multiple_of(((z + k + 2 * NZ) % NZ) * shard, shard), shard)

    w[b_own, slice_at(0), :hid] = gate[0]
    w[b_own, slice_at(0), hid : 2 * hid] = up[0]
    w[b_own, slice_at(0), 2 * hid :] = down[0].T

    experts = NX * NY * NC
    before = jnp.where(iota((n_tok, n_tok), 0) < iota((n_tok, n_tok), 1), 1.0, 0.0).astype(BF16)

    def slots_of(j):
        ids = iota((experts, n_tok), 0)
        member = jnp.zeros((experts, n_tok), jnp.bool_)
        weight = jnp.zeros((experts, n_tok), F32)
        for k in range(rout.shape[0]):
            hit = yr[j, k : k + 1, :] == ids
            member = member | hit
            weight = weight + jnp.where(hit, yc[j, k : k + 1, :], 0.0)
        count = jnp.dot(
            jnp.where(member, 1.0, 0.0).astype(BF16), before, preferred_element_type=F32
        )
        rank[j] = jnp.where(member, count, -1.0)
        scale[j] = weight

    yr[0] = rout[...]
    yc[0] = comb[...]
    yx[0] = tok[...]
    yg[0] = dout[...]
    slots_of(0)

    pl.semaphore_wait(barrier, 2 * (BLOCKS - 1) + 3)

    def swap_weights():
        return pltpu.make_async_remote_copy(
            src_ref=w.at[b_own, slice_at(0)],
            dst_ref=w.at[b_own, slice_at(0)],
            send_sem=sw_s.at[0],
            recv_sem=sw_r.at[0],
            device_id=partner,
            device_id_type=MESH,
        )

    def swap_weights_in():
        return pltpu.make_async_remote_copy(
            src_ref=w.at[b_oth, slice_at(0)],
            dst_ref=w.at[b_oth, slice_at(0)],
            send_sem=sw_s.at[0],
            recv_sem=sw_r.at[0],
            device_id=partner,
            device_id_type=MESH,
        )

    def gather_step(who, d, s, arriving=False):
        b = (b_own, b_oth)[who]
        sign = 1 if d == 0 else -1
        at = slice_at(-sign * (s + (1 if arriving else 0)))
        if s == STEPS - 1:
            half = shard // 2
            start = ((z - sign * (s + (1 if arriving else 0)) + 2 * NZ) % NZ) * shard
            at = pl.ds(pl.multiple_of(start + d * half, half), half)
        return pltpu.make_async_remote_copy(
            src_ref=w.at[b, at],
            dst_ref=w.at[b, at],
            send_sem=ag_s.at[who, d, s],
            recv_sem=ag_r.at[who, d, s],
            device_id=z_next(d),
            device_id_type=MESH,
        )

    def gather_next(who, s):
        for d in range(2):
            if s < STEPS:
                gather_step(who, d, s - 1, True).wait_recv()
                gather_step(who, d, s).start()

    def y_copy(j, a):
        return pltpu.make_async_remote_copy(
            src_ref=(rout, comb, tok, dout)[a],
            dst_ref=(yr, yc, yx, yg)[a].at[j],
            send_sem=sem_ys.at[j, a],
            recv_sem=sem_yr.at[j, a],
            device_id=(z, x * 16 + ((y + y_shift(j, c)) % 8) * 2 + c),
            device_id_type=MESH,
        )

    swap_weights().start()
    for d in range(2):
        gather_step(0, d, 0).start()
    for a in range(2):
        for j in Y_ORDER:
            y_copy(j, a).start()
    for j in Y_ORDER[:2]:
        y_copy(j, 2).start()
    for j in Y_ORDER[:2]:
        y_copy(j, 3).start()
    for a in (2, 3):
        y_copy(Y_ORDER[2], a).start()

    row = iota((3 * FULL, n_tok), 0)
    left_row = row % FULL
    is_hi = ((row // FULL) == 1) | (((row // FULL) == 2) & ((left_row % 4) >= 2))
    slot = jnp.where(row // FULL == 2, FULL + row % 2, row % FULL).astype(F32)
    q_row = iota((FULL, quarter), 0) // 4

    def pick_of(j, lo):
        chosen = jnp.where(is_hi, rank[j, pl.ds(lo + 8, 1), :], rank[j, pl.ds(lo, 1), :])
        return chosen == slot

    def store_block(dst, o, block):
        dst[o, :, :width] = block[:FULL].astype(BF16)
        dst[o, :, width:left] = block[FULL : 2 * FULL].astype(BF16)
        rest = block[2 * FULL :]
        packed = jnp.zeros((FULL, quarter), F32)
        for q in range(4):
            packed = jnp.where(q_row == q, rest[:, q * quarter : (q + 1) * quarter], packed)
        dst[o, :, left:] = packed.astype(BF16)

    def send_block(src, dst, o, s_sem, r_sem, to):
        pltpu.make_async_remote_copy(
            src_ref=src.at[o],
            dst_ref=dst.at[o],
            send_sem=s_sem,
            recv_sem=r_sem,
            device_id=to,
            device_id_type=MESH,
        ).start()

    def whole(src, dst, s_sem, r_sem, first):
        return pltpu.make_async_remote_copy(
            src_ref=src.at[pl.ds(first, BLOCKS - first)],
            dst_ref=dst.at[pl.ds(first, BLOCKS - first)],
            send_sem=s_sem,
            recv_sem=r_sem,
            device_id=partner,
            device_id_type=MESH,
        )

    def dispatch(j, scaled):
        rows_in, out, land = (yg, sg, rg) if scaled else (yx, sx, rx)
        s_sem, r_sem = (sem_gs, sem_gr) if scaled else (sem_xs, sem_xr)

        @pl.loop(0, 2)
        def _(dc):
            picks, scales = [], []
            for dx in X_ORDER:
                lo = ((x + dx) % 4) * 16 + (y % 4) * 2 + (c + dc) % 2
                hit = pick_of(j, lo)
                if scaled:
                    chosen = jnp.where(
                        is_hi, scale[j, pl.ds(lo + 8, 1), :], scale[j, pl.ds(lo, 1), :]
                    )
                    scales.append(jnp.sum(jnp.where(hit, chosen, 0.0), axis=1, keepdims=True))
                picks.append(jnp.where(hit, 1.0, 0.0).astype(BF16))
            block = jnp.dot(
                jnp.concatenate(picks, axis=0), rows_in[j], preferred_element_type=F32
            )
            if scaled:
                block = block * jnp.concatenate(scales, axis=0)
            for u, dx in enumerate(X_ORDER):
                o = (dx * 2 + dc) * 4 + j
                store_block(out, o, block[u * 3 * FULL : (u + 1) * 3 * FULL])
                to = (z, ((x + dx) % 4) * 16 + y * 2 + (c + dc) % 2)
                if dx:
                    send_block(out, land, o, s_sem, r_sem, to)
                else:

                    @pl.when(dc == 1)
                    def _():
                        send_block(out, land, o, s_sem, r_sem, to)

        land[j] = out[j]

    def own_picks():
        @pl.loop(0, BLOCKS)
        def _(o):
            xd, yd, cd = target(o)
            one_hot = jnp.where(
                pick_of(0, xd * 16 + (yd % 4) * 2 + cd), 1.0, 0.0
            ).astype(BF16)
            pick_lo[o] = one_hot[:FULL]
            pick_hi[o] = one_hot[FULL : 2 * FULL]
            pick_left[o] = one_hot[2 * FULL :]

    def rows_from(j, scaled):
        y_copy(j, 2 + scaled).wait_recv()
        dispatch(j, bool(scaled))

    dispatch(0, False)
    dispatch(0, True)
    for j in Y_ORDER:
        for a in range(2):
            y_copy(j, a).wait_recv()
        slots_of(j)
    gather_next(0, 1)
    rows_from(Y_ORDER[0], 0)
    rows_from(Y_ORDER[1], 0)
    swap_weights_in().wait_recv()
    for d in range(2):
        gather_step(1, d, 0).start()
    gather_next(0, 2)
    rows_from(Y_ORDER[0], 1)
    rows_from(Y_ORDER[1], 1)
    gather_next(1, 1)
    gather_next(0, 3)
    rows_from(Y_ORDER[2], 0)
    rows_from(Y_ORDER[2], 1)
    gather_next(1, 2)
    own_picks()
    gather_next(1, 3)

    def unpack(src, dst):
        for b in range(2):
            dst[b, :rows_main, :] = src[:, :, b * width : (b + 1) * width].reshape(
                rows_main, width
            )
        rest = src[:, :, left:].reshape(rows_main, quarter)
        r = iota((4 * BLOCKS, rows_main), 0)
        base = ((r % (2 * BLOCKS)) // 2) * FULL + (r // (2 * BLOCKS)) * 2 + r % 2
        for q in range(4):
            take = jnp.where(iota((4 * BLOCKS, rows_main), 1) == base + 4 * q, 1.0, 0.0)
            part_q = jnp.dot(take.astype(BF16), rest, preferred_element_type=F32).astype(BF16)
            for b in range(2):
                dst[b, rows_main:, q * quarter : (q + 1) * quarter] = part_q[
                    b * 2 * BLOCKS : (b + 1) * 2 * BLOCKS
                ]

    whole(sx, rx, sem_xs, sem_xr, NEAR).wait_recv()
    unpack(rx, xe)
    for who in range(2):
        for d in range(2):
            gather_step(who, d, STEPS - 1, True).wait_recv()

    chunk = 192

    def chunk_at(i):
        return pl.ds(pl.multiple_of(i * chunk, chunk), chunk)

    def forward_rows(b):
        @pl.loop(0, rows_all // chunk)
        def _(i):
            at = chunk_at(i)
            pre[b, at, :] = jnp.dot(xe[b, at, :], w[b, :, : 2 * hid], preferred_element_type=F32)

    def backward_rows(b):
        @pl.loop(0, rows_all // chunk)
        def _(i):
            at = chunk_at(i)
            d_hidden = jnp.dot(ge[b, at, :], w[b, :, 2 * hid :], preferred_element_type=F32)
            gate_pre, up_pre = pre[b, at, :hid], pre[b, at, hid:]
            sig = jax.nn.sigmoid(gate_pre)
            silu = gate_pre * sig
            d_gate = d_hidden * up_pre * sig * (1.0 + gate_pre * (1.0 - sig))
            dph[b, at, :hid] = d_gate.astype(BF16)
            dph[b, at, hid : 2 * hid] = (d_hidden * silu).astype(BF16)
            dph[b, at, 2 * hid :] = (silu * up_pre).astype(BF16)

    def input_rows(b):
        @pl.loop(0, rows_all // chunk)
        def _(i):
            at = chunk_at(i)
            dr[b, at, :] = dot_nt(dph[b, at, : 2 * hid], w[b, :, : 2 * hid]).astype(BF16)

    def grads_of(b):
        for k in range(3):
            src = xe if k < 2 else ge
            total = dot_tn(dph[b, :, k * hid : (k + 1) * hid], src[b]).astype(BF16)
            for s in range(NZ):
                wg[b, s, k * hid : (k + 1) * hid, :] = total[:, s * shard : (s + 1) * shard]

    half_rows = 3 * hid // 2

    def red_step(who, d, s):
        b = (b_own, b_oth)[who]
        sign = 1 if d == 0 else -1
        k = STEPS - s
        span = pl.ds(d * half_rows, half_rows) if s == 0 else pl.ds(0, 2 * half_rows)
        return pltpu.make_async_remote_copy(
            src_ref=wg.at[b, (z + sign * k + NZ) % NZ, span],
            dst_ref=part.at[who, d, s, span],
            send_sem=red_s.at[who, d, s],
            recv_sem=red_r.at[who, d, s],
            device_id=z_next(d),
            device_id_type=MESH,
        )

    def red_next(who, s):
        b = (b_own, b_oth)[who]
        for d in range(2):
            if s < STEPS:
                sign = 1 if d == 0 else -1
                at = (z + sign * (STEPS - s) + NZ) % NZ
                red_step(who, d, s - 1).wait_recv()
                span = pl.ds(d * half_rows, half_rows) if s == 1 else pl.ds(0, 2 * half_rows)
                wg[b, at, span, :] = (
                    wg[b, at, span, :].astype(F32) + part[who, d, s - 1, span, :].astype(F32)
                ).astype(BF16)
                red_step(who, d, s).start()

    @pl.loop(0, 2)
    def _(b):
        forward_rows(b)

    whole(sg, rg, sem_gs, sem_gr, NEAR).wait_recv()
    unpack(rg, ge)

    for who in (1, 0):
        b = (b_own, b_oth)[who]
        backward_rows(b)
        grads_of(b)
        if who == 0:
            red_next(1, 1)
        for d in range(2):
            red_step(who, d, 0).start()

    @pl.loop(0, 2)
    def _(b):
        input_rows(b)

    for b in range(2):
        sr[:, :, b * width : (b + 1) * width] = dr[b, :rows_main, :].reshape(BLOCKS, FULL, width)
    spread_row = iota((rows_main, 4 * BLOCKS), 0)
    spread = jnp.where(
        iota((rows_main, 4 * BLOCKS), 1)
        == ((spread_row // 2) % 2) * 2 * BLOCKS + (spread_row // FULL) * 2 + spread_row % 2,
        1.0,
        0.0,
    ).astype(BF16)
    tails = jnp.concatenate([dr[0, rows_main:, :], dr[1, rows_main:, :]], axis=0)
    tails = jnp.dot(spread, tails, preferred_element_type=F32)
    q_all = (iota((rows_main, quarter), 0) // 4) % 4
    packed = jnp.zeros((rows_main, quarter), F32)
    for q in range(4):
        packed = jnp.where(q_all == q, tails[:, q * quarter : (q + 1) * quarter], packed)
    sr[:, :, left:] = packed.astype(BF16).reshape(BLOCKS, FULL, quarter)

    @pl.loop(0, BLOCKS - 1)
    def _(i):
        o = block_at((i + SELF + 1) % BLOCKS)
        send_block(sr, rr, o, sem_rs, sem_rr, backward(o))

    rr[0] = sr[0]

    red_next(1, 2)
    red_next(0, 1)
    red_next(1, 3)
    red_next(0, 2)

    def final(who):
        b = (b_own, b_oth)[who]
        total = wg[b, z].astype(F32)
        for d in range(2):
            last = STEPS - 1
            red_step(who, d, last).wait_recv()
            total = total + part[who, d, last].astype(F32)
        return total

    swap[...] = final(1).astype(BF16)
    swap_grads = pltpu.make_async_remote_copy(
        src_ref=swap,
        dst_ref=swap_in,
        send_sem=sw_s.at[1],
        recv_sem=sw_r.at[1],
        device_id=partner,
        device_id_type=MESH,
    )
    swap_grads.start()
    red_next(0, 3)

    whole(sr, rr, sem_rs, sem_rr, 1).wait_recv()
    d_tok = dot_tn(
        pick_lo[...].reshape(rows_main, n_tok), rr[:, :, :width].reshape(rows_main, width)
    ) + dot_tn(
        pick_hi[...].reshape(rows_main, n_tok), rr[:, :, width:left].reshape(rows_main, width)
    )
    tail_pick = pick_left[...].reshape(rows_main, n_tok)
    tail = rr[:, :, left:].reshape(rows_main, quarter)
    q_pick = (iota((rows_main, n_tok), 0) // 4) % 4
    for q in range(4):
        one = jnp.where(q_pick == q, tail_pick.astype(F32), 0.0).astype(BF16)
        o_tok[:, q * quarter : (q + 1) * quarter] = (
            d_tok[:, q * quarter : (q + 1) * quarter] + dot_tn(one, tail)
        ).astype(BF16)

    total = final(0)
    swap_grads.wait_recv()
    total = total + swap_in[...].astype(F32)
    o_gate[0] = total[:hid].T
    o_up[0] = total[hid : 2 * hid].T
    o_down[0] = total[2 * hid :]

    whole(sx, rx, sem_xs, sem_xr, NEAR).wait_send()
    whole(sg, rg, sem_gs, sem_gr, NEAR).wait_send()
    whole(sr, rr, sem_rs, sem_rr, 1).wait_send()
    swap_weights().wait_send()
    for j in Y_ORDER:
        for a in range(4):
            y_copy(j, a).wait_send()
    swap_grads.wait_send()
    for who in range(2):
        for d in range(2):
            for s in range(STEPS):
                gather_step(who, d, s).wait_send()
                red_step(who, d, s).wait_send()


def body(tokens, d_output, combine, routes, gate_weight, up_weight, down_weight):
    n_tok, width = tokens.shape
    hid = gate_weight.shape[2]
    top = routes.shape[1]
    shard = width // NZ
    block = (BLOCKS, FULL, 2 * width + width // 4)
    rows = BLOCKS * CAP
    vmem = pl.BlockSpec(memory_space=pltpu.VMEM)
    dma = pltpu.SemaphoreType.DMA
    return pl.pallas_call(
        kernel,
        out_shape=(
            jax.ShapeDtypeStruct((n_tok, width), BF16),
            jax.ShapeDtypeStruct((1, shard, hid), F32),
            jax.ShapeDtypeStruct((1, shard, hid), F32),
            jax.ShapeDtypeStruct((1, hid, shard), F32),
        ),
        in_specs=[vmem] * 7,
        out_specs=(vmem,) * 4,
        scratch_shapes=[
            pltpu.VMEM((4, NX * NY * NC, n_tok), F32),
            pltpu.VMEM((4, NX * NY * NC, n_tok), F32),
            pltpu.VMEM((4, top, n_tok), jnp.int32),
            pltpu.VMEM((4, top, n_tok), F32),
            pltpu.VMEM((4, n_tok, width), BF16),
            pltpu.VMEM((4, n_tok, width), BF16),
            pltpu.VMEM((BLOCKS, FULL, n_tok), BF16),
            pltpu.VMEM((BLOCKS, FULL, n_tok), BF16),
            pltpu.VMEM((BLOCKS, FULL, n_tok), BF16),
            pltpu.VMEM((2, width, 3 * hid), BF16),
            pltpu.VMEM(block, BF16),
            pltpu.VMEM(block, BF16),
            pltpu.VMEM(block, BF16),
            pltpu.VMEM(block, BF16),
            pltpu.VMEM((2, rows, width), BF16),
            pltpu.VMEM((2, rows, width), BF16),
            pltpu.VMEM((2, rows, width), BF16),
            pltpu.VMEM((2, rows, 2 * hid), F32),
            pltpu.VMEM((2, rows, 3 * hid), BF16),
            pltpu.VMEM(block, BF16),
            pltpu.VMEM(block, BF16),
            pltpu.VMEM((2, NZ, 3 * hid, shard), BF16),
            pltpu.VMEM((2, 2, 4, 3 * hid, shard), BF16),
            pltpu.VMEM((3 * hid, shard), BF16),
            pltpu.VMEM((3 * hid, shard), BF16),
            dma,
            dma,
            dma,
            dma,
            dma,
            dma,
            dma((4, 4)),
            dma((4, 4)),
            dma((2, 2, 4)),
            dma((2, 2, 4)),
            dma((2, 2, 4)),
            dma((2, 2, 4)),
            dma((2,)),
            dma((2,)),
        ],
        compiler_params=pltpu.CompilerParams(
            collective_id=0, has_side_effects=True, vmem_limit_bytes=56 << 20
        ),
        name="moe_backward",
    )(tokens, d_output, combine.T, routes.T, gate_weight, up_weight, down_weight)


def solution(mesh):
    placed = (
        P(("dp", "expert"), None),
        P(("dp", "expert"), None),
        P(("dp", "expert"), None),
        P(("dp", "expert"), None),
        P("expert", "dp", None),
        P("expert", "dp", None),
        P("expert", None, "dp"),
    )
    return jax.shard_map(
        body,
        mesh=mesh,
        in_specs=placed,
        out_specs=(
            P(("dp", "expert"), None),
            P("expert", "dp", None),
            P("expert", "dp", None),
            P("expert", None, "dp"),
        ),
        check_vma=False,
    )
```

```python
import functools

import jax
import jax.numpy as jnp
from jax import lax
from jax.experimental import pallas as pl
from jax.experimental.pallas import tpu as pltpu
from jax.sharding import PartitionSpec as P

MESH = pl.DeviceIdType.MESH
F32 = jnp.float32
BF16 = jnp.bfloat16

NX, NY, NC, NZ = 4, 8, 2, 8
BLOCKS = 32
FULL = 16
CAP = 18
SELF = 3
NEAR = 4
Y_ORDER = (1, 3, 2)
X_ORDER = (2, 1, 3, 0)
STEPS = 4


def iota(shape, dim):
    return lax.broadcasted_iota(jnp.int32, shape, dim)


def y_shift(j, core):
    return j + 4 * (j // 3) + 4 * core * ((j // 2) % 2) * ((j + 1) % 2)


def far_first(k):
    return (2 + k) * (1 - k // 2) + (3 - k) * (k // 2)


def block_at(i):
    dx = far_first(i % 4)
    j = (dx + 4 - (i // 4) % 4) % 4
    return (dx * 2 + i // 16) * 4 + j


def dot_tn(a, b):
    return lax.dot_general(a, b, (((0,), (0,)), ((), ())), preferred_element_type=F32)


def dot_nt(a, b):
    return lax.dot_general(a, b, (((1,), (1,)), ((), ())), preferred_element_type=F32)


def kernel(
    tok,
    dout,
    comb,
    rout,
    gate,
    up,
    down,
    o_tok,
    o_gate,
    o_up,
    o_down,
    rank,
    scale,
    yr,
    yc,
    yx,
    yg,
    pick_lo,
    pick_hi,
    pick_left,
    w,
    sx,
    sg,
    rx,
    rg,
    xe,
    ge,
    dr,
    pre,
    dph,
    sr,
    rr,
    wg,
    part,
    swap,
    swap_in,
    sem_xs,
    sem_xr,
    sem_gs,
    sem_gr,
    sem_rs,
    sem_rr,
    sem_ys,
    sem_yr,
    ag_s,
    ag_r,
    red_s,
    red_r,
    sw_s,
    sw_r,
):
    z = lax.axis_index("dp")
    e = lax.axis_index("expert")
    x, y, c = e // 16, (e // 2) % 8, e % 2
    b_own = y // 4
    b_oth = 1 - b_own
    n_tok, width = tok.shape
    hid = gate.shape[2]
    shard = width // NZ
    left = 2 * width
    quarter = width // 4
    rows_main = BLOCKS * FULL
    rows_all = BLOCKS * CAP
    partner = (z, x * 16 + ((y + 4) % 8) * 2 + c)

    def target(o):
        dx, j, dc = o // 8, o % 4, (o // 4) % 2
        return (x + dx) % 4, (y + y_shift(j, c)) % 8, (c + dc) % 2

    def forward(o):
        xd, yd, cd = target(o)
        return (z, xd * 16 + yd * 2 + cd)

    def backward(o):
        dx, j, dc = o // 8, o % 4, (o // 4) % 2
        cs = (c + dc) % 2
        return (z, ((x + 4 - dx) % 4) * 16 + ((y + 8 - y_shift(j, cs)) % 8) * 2 + cs)

    def z_next(d):
        return ((z + (1 if d == 0 else NZ - 1)) % NZ, e)

    barrier = pltpu.get_barrier_semaphore()

    @pl.loop(1, BLOCKS)
    def _(o):
        pl.semaphore_signal(barrier, inc=1, device_id=forward(o), device_id_type=MESH)
        pl.semaphore_signal(barrier, inc=1, device_id=backward(o), device_id_type=MESH)

    for d in range(2):
        pl.semaphore_signal(barrier, inc=1, device_id=z_next(d), device_id_type=MESH)
    pl.semaphore_signal(barrier, inc=1, device_id=partner, device_id_type=MESH)

    def slice_at(k):
        return pl.ds(pl.multiple_of(((z + k + 2 * NZ) % NZ) * shard, shard), shard)

    w[b_own, slice_at(0), :hid] = gate[0]
    w[b_own, slice_at(0), hid : 2 * hid] = up[0]
    w[b_own, slice_at(0), 2 * hid :] = down[0].T

    experts = NX * NY * NC
    before = jnp.where(iota((n_tok, n_tok), 0) < iota((n_tok, n_tok), 1), 1.0, 0.0).astype(BF16)

    def slots_of(j):
        ids = iota((experts, n_tok), 0)
        member = jnp.zeros((experts, n_tok), jnp.bool_)
        weight = jnp.zeros((experts, n_tok), F32)
        for k in range(rout.shape[0]):
            hit = yr[j, k : k + 1, :] == ids
            member = member | hit
            weight = weight + jnp.where(hit, yc[j, k : k + 1, :], 0.0)
        count = jnp.dot(
            jnp.where(member, 1.0, 0.0).astype(BF16), before, preferred_element_type=F32
        )
        rank[j] = jnp.where(member, count, -1.0)
        scale[j] = weight

    yr[0] = rout[...]
    yc[0] = comb[...]
    yx[0] = tok[...]
    yg[0] = dout[...]
    slots_of(0)

    pl.semaphore_wait(barrier, 2 * (BLOCKS - 1) + 3)

    def swap_weights():
        return pltpu.make_async_remote_copy(
            src_ref=w.at[b_own, slice_at(0)],
            dst_ref=w.at[b_own, slice_at(0)],
            send_sem=sw_s.at[0],
            recv_sem=sw_r.at[0],
            device_id=partner,
            device_id_type=MESH,
        )

    def swap_weights_in():
        return pltpu.make_async_remote_copy(
            src_ref=w.at[b_oth, slice_at(0)],
            dst_ref=w.at[b_oth, slice_at(0)],
            send_sem=sw_s.at[0],
            recv_sem=sw_r.at[0],
            device_id=partner,
            device_id_type=MESH,
        )

    def gather_step(who, d, s, arriving=False):
        b = (b_own, b_oth)[who]
        sign = 1 if d == 0 else -1
        at = slice_at(-sign * (s + (1 if arriving else 0)))
        if s == STEPS - 1:
            half = shard // 2
            start = ((z - sign * (s + (1 if arriving else 0)) + 2 * NZ) % NZ) * shard
            at = pl.ds(pl.multiple_of(start + d * half, half), half)
        return pltpu.make_async_remote_copy(
            src_ref=w.at[b, at],
            dst_ref=w.at[b, at],
            send_sem=ag_s.at[who, d, s],
            recv_sem=ag_r.at[who, d, s],
            device_id=z_next(d),
            device_id_type=MESH,
        )

    def gather_next(who, s):
        for d in range(2):
            if s < STEPS:
                gather_step(who, d, s - 1, True).wait_recv()
                gather_step(who, d, s).start()

    def y_copy(j, a):
        return pltpu.make_async_remote_copy(
            src_ref=(rout, comb, tok, dout)[a],
            dst_ref=(yr, yc, yx, yg)[a].at[j],
            send_sem=sem_ys.at[j, a],
            recv_sem=sem_yr.at[j, a],
            device_id=(z, x * 16 + ((y + y_shift(j, c)) % 8) * 2 + c),
            device_id_type=MESH,
        )

    swap_weights().start()
    for d in range(2):
        gather_step(0, d, 0).start()
    for a in range(2):
        for j in Y_ORDER:
            y_copy(j, a).start()
    for j in Y_ORDER[:2]:
        y_copy(j, 2).start()
    for j in Y_ORDER[:2]:
        y_copy(j, 3).start()
    for a in (2, 3):
        y_copy(Y_ORDER[2], a).start()

    row = iota((3 * FULL, n_tok), 0)
    left_row = row % FULL
    is_hi = ((row // FULL) == 1) | (((row // FULL) == 2) & ((left_row % 4) >= 2))
    slot = jnp.where(row // FULL == 2, FULL + row % 2, row % FULL).astype(F32)
    q_row = iota((FULL, quarter), 0) // 4

    def pick_of(j, lo):
        chosen = jnp.where(is_hi, rank[j, pl.ds(lo + 8, 1), :], rank[j, pl.ds(lo, 1), :])
        return chosen == slot

    def store_block(dst, o, block):
        dst[o, :, :width] = block[:FULL].astype(BF16)
        dst[o, :, width:left] = block[FULL : 2 * FULL].astype(BF16)
        rest = block[2 * FULL :]
        packed = jnp.zeros((FULL, quarter), F32)
        for q in range(4):
            packed = jnp.where(q_row == q, rest[:, q * quarter : (q + 1) * quarter], packed)
        dst[o, :, left:] = packed.astype(BF16)

    def send_block(src, dst, o, s_sem, r_sem, to):
        pltpu.make_async_remote_copy(
            src_ref=src.at[o],
            dst_ref=dst.at[o],
            send_sem=s_sem,
            recv_sem=r_sem,
            device_id=to,
            device_id_type=MESH,
        ).start()

    def whole(src, dst, s_sem, r_sem, first):
        return pltpu.make_async_remote_copy(
            src_ref=src.at[pl.ds(first, BLOCKS - first)],
            dst_ref=dst.at[pl.ds(first, BLOCKS - first)],
            send_sem=s_sem,
            recv_sem=r_sem,
            device_id=partner,
            device_id_type=MESH,
        )

    def dispatch(j, scaled):
        rows_in, out, land = (yg, sg, rg) if scaled else (yx, sx, rx)
        s_sem, r_sem = (sem_gs, sem_gr) if scaled else (sem_xs, sem_xr)

        @pl.loop(0, 2)
        def _(dc):
            picks, scales = [], []
            for dx in X_ORDER:
                lo = ((x + dx) % 4) * 16 + (y % 4) * 2 + (c + dc) % 2
                hit = pick_of(j, lo)
                if scaled:
                    chosen = jnp.where(
                        is_hi, scale[j, pl.ds(lo + 8, 1), :], scale[j, pl.ds(lo, 1), :]
                    )
                    scales.append(jnp.sum(jnp.where(hit, chosen, 0.0), axis=1, keepdims=True))
                picks.append(jnp.where(hit, 1.0, 0.0).astype(BF16))
            block = jnp.dot(
                jnp.concatenate(picks, axis=0), rows_in[j], preferred_element_type=F32
            )
            if scaled:
                block = block * jnp.concatenate(scales, axis=0)
            for u, dx in enumerate(X_ORDER):
                o = (dx * 2 + dc) * 4 + j
                store_block(out, o, block[u * 3 * FULL : (u + 1) * 3 * FULL])
                to = (z, ((x + dx) % 4) * 16 + y * 2 + (c + dc) % 2)
                if dx:
                    send_block(out, land, o, s_sem, r_sem, to)
                else:

                    @pl.when(dc == 1)
                    def _():
                        send_block(out, land, o, s_sem, r_sem, to)

        land[j] = out[j]

    def own_picks():
        @pl.loop(0, BLOCKS)
        def _(o):
            xd, yd, cd = target(o)
            one_hot = jnp.where(
                pick_of(0, xd * 16 + (yd % 4) * 2 + cd), 1.0, 0.0
            ).astype(BF16)
            pick_lo[o] = one_hot[:FULL]
            pick_hi[o] = one_hot[FULL : 2 * FULL]
            pick_left[o] = one_hot[2 * FULL :]

    def rows_from(j, scaled):
        y_copy(j, 2 + scaled).wait_recv()
        dispatch(j, bool(scaled))

    dispatch(0, False)
    dispatch(0, True)
    for j in Y_ORDER:
        for a in range(2):
            y_copy(j, a).wait_recv()
        slots_of(j)
    gather_next(0, 1)
    rows_from(Y_ORDER[0], 0)
    rows_from(Y_ORDER[1], 0)
    swap_weights_in().wait_recv()
    for d in range(2):
        gather_step(1, d, 0).start()
    gather_next(0, 2)
    rows_from(Y_ORDER[0], 1)
    rows_from(Y_ORDER[1], 1)
    gather_next(1, 1)
    gather_next(0, 3)
    rows_from(Y_ORDER[2], 0)
    rows_from(Y_ORDER[2], 1)
    gather_next(1, 2)
    own_picks()
    gather_next(1, 3)

    def unpack_full(src, dst, b):
        lanes = pl.ds(pl.multiple_of(b * width, width), width)
        dst[b, :rows_main, :] = src[:, :, lanes].reshape(rows_main, width)

    def unpack_rest(src, dst):
        rest = src[:, :, left:].reshape(rows_main, quarter)
        r = iota((4 * BLOCKS, rows_main), 0)
        base = ((r % (2 * BLOCKS)) // 2) * FULL + (r // (2 * BLOCKS)) * 2 + r % 2
        for q in range(4):
            take = jnp.where(iota((4 * BLOCKS, rows_main), 1) == base + 4 * q, 1.0, 0.0)
            part_q = jnp.dot(take.astype(BF16), rest, preferred_element_type=F32).astype(BF16)
            for b in range(2):
                dst[b, rows_main:, q * quarter : (q + 1) * quarter] = part_q[
                    b * 2 * BLOCKS : (b + 1) * 2 * BLOCKS
                ]

    whole(sx, rx, sem_xs, sem_xr, NEAR).wait_recv()
    unpack_rest(rx, xe)
    for b in range(2):
        unpack_full(rx, xe, b)
    for who in range(2):
        for d in range(2):
            gather_step(who, d, STEPS - 1, True).wait_recv()

    chunk = 192

    def chunk_at(i):
        return pl.ds(pl.multiple_of(i * chunk, chunk), chunk)

    def forward_rows(b):
        @pl.loop(0, rows_all // chunk)
        def _(i):
            at = chunk_at(i)
            pre[b, at, :] = jnp.dot(xe[b, at, :], w[b, :, : 2 * hid], preferred_element_type=F32)

    def backward_rows(b):
        @pl.loop(0, rows_all // chunk)
        def _(i):
            at = chunk_at(i)
            d_hidden = jnp.dot(ge[b, at, :], w[b, :, 2 * hid :], preferred_element_type=F32)
            gate_pre, up_pre = pre[b, at, :hid], pre[b, at, hid:]
            sig = jax.nn.sigmoid(gate_pre)
            silu = gate_pre * sig
            d_gate = d_hidden * up_pre * sig * (1.0 + gate_pre * (1.0 - sig))
            dph[b, at, :hid] = d_gate.astype(BF16)
            dph[b, at, hid : 2 * hid] = (d_hidden * silu).astype(BF16)
            dph[b, at, 2 * hid :] = (silu * up_pre).astype(BF16)

    def input_rows(b):
        @pl.loop(0, rows_all // chunk)
        def _(i):
            at = chunk_at(i)
            dr[b, at, :] = dot_nt(dph[b, at, : 2 * hid], w[b, :, : 2 * hid]).astype(BF16)

    def grads_of(b):
        for k in range(3):
            src = xe if k < 2 else ge
            total = dot_tn(dph[b, :, k * hid : (k + 1) * hid], src[b]).astype(BF16)
            for s in range(NZ):
                wg[b, s, k * hid : (k + 1) * hid, :] = total[:, s * shard : (s + 1) * shard]

    half_rows = 3 * hid // 2

    def red_step(who, d, s):
        b = (b_own, b_oth)[who]
        sign = 1 if d == 0 else -1
        k = STEPS - s
        span = pl.ds(d * half_rows, half_rows) if s == 0 else pl.ds(0, 2 * half_rows)
        return pltpu.make_async_remote_copy(
            src_ref=wg.at[b, (z + sign * k + NZ) % NZ, span],
            dst_ref=part.at[who, d, s, span],
            send_sem=red_s.at[who, d, s],
            recv_sem=red_r.at[who, d, s],
            device_id=z_next(d),
            device_id_type=MESH,
        )

    def red_next(who, s):
        b = (b_own, b_oth)[who]
        for d in range(2):
            if s < STEPS:
                sign = 1 if d == 0 else -1
                at = (z + sign * (STEPS - s) + NZ) % NZ
                red_step(who, d, s - 1).wait_recv()
                span = pl.ds(d * half_rows, half_rows) if s == 1 else pl.ds(0, 2 * half_rows)
                wg[b, at, span, :] = (
                    wg[b, at, span, :].astype(F32) + part[who, d, s - 1, span, :].astype(F32)
                ).astype(BF16)
                red_step(who, d, s).start()

    @pl.loop(0, 2)
    def _(b):
        forward_rows(b)

    whole(sg, rg, sem_gs, sem_gr, NEAR).wait_recv()
    unpack_rest(rg, ge)

    for who in (1, 0):
        b = (b_own, b_oth)[who]
        unpack_full(rg, ge, b)
        backward_rows(b)
        grads_of(b)
        if who == 0:
            red_next(1, 1)
        for d in range(2):
            red_step(who, d, 0).start()

    @pl.loop(0, 2)
    def _(b):
        input_rows(b)

    for b in range(2):
        sr[:, :, b * width : (b + 1) * width] = dr[b, :rows_main, :].reshape(BLOCKS, FULL, width)
    spread_row = iota((rows_main, 4 * BLOCKS), 0)
    spread = jnp.where(
        iota((rows_main, 4 * BLOCKS), 1)
        == ((spread_row // 2) % 2) * 2 * BLOCKS + (spread_row // FULL) * 2 + spread_row % 2,
        1.0,
        0.0,
    ).astype(BF16)
    tails = jnp.concatenate([dr[0, rows_main:, :], dr[1, rows_main:, :]], axis=0)
    tails = jnp.dot(spread, tails, preferred_element_type=F32)
    q_all = (iota((rows_main, quarter), 0) // 4) % 4
    packed = jnp.zeros((rows_main, quarter), F32)
    for q in range(4):
        packed = jnp.where(q_all == q, tails[:, q * quarter : (q + 1) * quarter], packed)
    sr[:, :, left:] = packed.astype(BF16).reshape(BLOCKS, FULL, quarter)

    @pl.loop(0, BLOCKS - 1)
    def _(i):
        o = block_at((i + SELF + 1) % BLOCKS)
        send_block(sr, rr, o, sem_rs, sem_rr, backward(o))

    rr[0] = sr[0]

    red_next(1, 2)
    red_next(0, 1)
    red_next(1, 3)
    red_next(0, 2)

    def final(who):
        b = (b_own, b_oth)[who]
        total = wg[b, z].astype(F32)
        for d in range(2):
            last = STEPS - 1
            red_step(who, d, last).wait_recv()
            total = total + part[who, d, last].astype(F32)
        return total

    swap[...] = final(1).astype(BF16)
    swap_grads = pltpu.make_async_remote_copy(
        src_ref=swap,
        dst_ref=swap_in,
        send_sem=sw_s.at[1],
        recv_sem=sw_r.at[1],
        device_id=partner,
        device_id_type=MESH,
    )
    swap_grads.start()
    red_next(0, 3)

    whole(sr, rr, sem_rs, sem_rr, 1).wait_recv()
    d_tok = dot_tn(
        pick_lo[...].reshape(rows_main, n_tok), rr[:, :, :width].reshape(rows_main, width)
    ) + dot_tn(
        pick_hi[...].reshape(rows_main, n_tok), rr[:, :, width:left].reshape(rows_main, width)
    )
    tail_pick = pick_left[...].reshape(rows_main, n_tok)
    tail = rr[:, :, left:].reshape(rows_main, quarter)
    q_pick = (iota((rows_main, n_tok), 0) // 4) % 4
    for q in range(4):
        one = jnp.where(q_pick == q, tail_pick.astype(F32), 0.0).astype(BF16)
        o_tok[:, q * quarter : (q + 1) * quarter] = (
            d_tok[:, q * quarter : (q + 1) * quarter] + dot_tn(one, tail)
        )

    total = final(0)
    swap_grads.wait_recv()
    total = total + swap_in[...].astype(F32)
    o_gate[0] = total[:hid].T
    o_up[0] = total[hid : 2 * hid].T
    o_down[0] = total[2 * hid :]

    whole(sx, rx, sem_xs, sem_xr, NEAR).wait_send()
    whole(sg, rg, sem_gs, sem_gr, NEAR).wait_send()
    whole(sr, rr, sem_rs, sem_rr, 1).wait_send()
    swap_weights().wait_send()
    for j in Y_ORDER:
        for a in range(4):
            y_copy(j, a).wait_send()
    swap_grads.wait_send()
    for who in range(2):
        for d in range(2):
            for s in range(STEPS):
                gather_step(who, d, s).wait_send()
                red_step(who, d, s).wait_send()


def body(tokens, d_output, combine, routes, gate_weight, up_weight, down_weight):
    n_tok, width = tokens.shape
    hid = gate_weight.shape[2]
    top = routes.shape[1]
    shard = width // NZ
    block = (BLOCKS, FULL, 2 * width + width // 4)
    rows = BLOCKS * CAP
    vmem = pl.BlockSpec(memory_space=pltpu.VMEM)
    dma = pltpu.SemaphoreType.DMA
    d_tokens, d_gate, d_up, d_down = pl.pallas_call(
        kernel,
        out_shape=(
            jax.ShapeDtypeStruct((n_tok, width), F32),
            jax.ShapeDtypeStruct((1, shard, hid), F32),
            jax.ShapeDtypeStruct((1, shard, hid), F32),
            jax.ShapeDtypeStruct((1, hid, shard), F32),
        ),
        in_specs=[vmem] * 7,
        out_specs=(vmem,) * 4,
        scratch_shapes=[
            pltpu.VMEM((4, NX * NY * NC, n_tok), F32),
            pltpu.VMEM((4, NX * NY * NC, n_tok), F32),
            pltpu.VMEM((4, top, n_tok), jnp.int32),
            pltpu.VMEM((4, top, n_tok), F32),
            pltpu.VMEM((4, n_tok, width), BF16),
            pltpu.VMEM((4, n_tok, width), BF16),
            pltpu.VMEM((BLOCKS, FULL, n_tok), BF16),
            pltpu.VMEM((BLOCKS, FULL, n_tok), BF16),
            pltpu.VMEM((BLOCKS, FULL, n_tok), BF16),
            pltpu.VMEM((2, width, 3 * hid), BF16),
            pltpu.VMEM(block, BF16),
            pltpu.VMEM(block, BF16),
            pltpu.VMEM(block, BF16),
            pltpu.VMEM(block, BF16),
            pltpu.VMEM((2, rows, width), BF16),
            pltpu.VMEM((2, rows, width), BF16),
            pltpu.VMEM((2, rows, width), BF16),
            pltpu.VMEM((2, rows, 2 * hid), F32),
            pltpu.VMEM((2, rows, 3 * hid), BF16),
            pltpu.VMEM(block, BF16),
            pltpu.VMEM(block, BF16),
            pltpu.VMEM((2, NZ, 3 * hid, shard), BF16),
            pltpu.VMEM((2, 2, 4, 3 * hid, shard), BF16),
            pltpu.VMEM((3 * hid, shard), BF16),
            pltpu.VMEM((3 * hid, shard), BF16),
            dma,
            dma,
            dma,
            dma,
            dma,
            dma,
            dma((4, 4)),
            dma((4, 4)),
            dma((2, 2, 4)),
            dma((2, 2, 4)),
            dma((2, 2, 4)),
            dma((2, 2, 4)),
            dma((2,)),
            dma((2,)),
        ],
        compiler_params=pltpu.CompilerParams(
            collective_id=0, has_side_effects=True, vmem_limit_bytes=56 << 20
        ),
        name="moe_backward",
    )(tokens, d_output, combine.T, routes.T, gate_weight, up_weight, down_weight)
    return d_tokens.astype(BF16), d_gate, d_up, d_down


def solution(mesh):
    placed = (
        P(("dp", "expert"), None),
        P(("dp", "expert"), None),
        P(("dp", "expert"), None),
        P(("dp", "expert"), None),
        P("expert", "dp", None),
        P("expert", "dp", None),
        P("expert", None, "dp"),
    )
    return jax.shard_map(
        body,
        mesh=mesh,
        in_specs=placed,
        out_specs=(
            P(("dp", "expert"), None),
            P("expert", "dp", None),
            P("expert", "dp", None),
            P("expert", None, "dp"),
        ),
        check_vma=False,
    )
```
